256 devices in a mesh: chain: 8 (over x, core), col: 32 (over y, z).
Axes of the slice: x: 4, y: 4, z: 8, core: 2. Of those that a mesh axis runs over, the one named last changes fastest.
Arguments:
- rhs: float32 [8, 32, 64, 128], P('chain', 'col'), may hold values from -6 to 6
- inverse: float32 [8, 32, 128, 128], P('chain', 'col'), as said below
- factor: float32 [8, 32, 8, 128, 128], P('chain', 'col'), may hold values from -0.1875 to 0.1875
- pattern: int32 [8, 32, 8], P('chain', 'col'), may hold values from 0 to 31, as said below
Outputs:
- forward: float32 [8, 32, 64, 128], P('chain', 'col')
- solution: float32 [8, 32, 64, 128], P('chain', 'col')
The draws below stay inside these ranges and needn't reach their ends.
Inputs may be any that keep to these rules, and one draw needn't show every extreme that they name: `pattern`: the 8 block rows of one supernode are distinct. `inverse`: each block is lower triangular, its diagonal between 0.5 and 1.5.
All inputs are finite; a program needn't handle non-finite values.
Results may differ from the reference program's by a relative error of at most 0.00012.
Values sent between devices are 32-bit elements; how exact they have to be, the bound alone decides.
No kernel may reach another device: no remote copies, remote signals or barrier semaphores. Data moves between devices by JAX's collectives and lax.ppermute only.
A program may use at most 64 MiB of HBM per device.

```python
import jax
import jax.numpy as jnp
from jax import lax

BLOCK = 128
NB = 8
LOADS = 64
LEVELS = 8
SUPS = 32


def draw_inverse(key, part):
    keyed = jax.random.fold_in(key, 7)
    first, second = jax.random.split(keyed)
    diagonal = jax.random.uniform(first, (LEVELS, SUPS, BLOCK), jnp.float32, 0.5, 1.5)
    lower = jax.random.normal(second, (LEVELS, SUPS, BLOCK, BLOCK), jnp.float32) * (0.6 / BLOCK ** 0.5)
    strict = jnp.tril(jnp.ones((BLOCK, BLOCK), jnp.float32), -1)
    return lower * strict + diagonal[..., None] * jnp.eye(BLOCK, dtype=jnp.float32)


def draw_pattern(key, part):
    keyed = jax.random.fold_in(key, 11)
    keys = jax.random.split(keyed, LEVELS * SUPS)
    chosen = jax.vmap(lambda single: jax.random.permutation(single, SUPS)[:NB])(keys)
    return chosen.reshape(LEVELS, SUPS, NB).astype(jnp.int32)


def block_levels(own_key, extent, cuts, smallest, high):
    gain = 1.0
    for axis_at, shards_of in cuts:
        draws = jax.random.uniform(jax.random.fold_in(jax.random.fold_in(own_key, 6), axis_at), (shards_of,), jnp.float32, smallest / len(cuts), high / len(cuts))
        gain = gain * jnp.repeat(jnp.exp(draws), extent[axis_at] // shards_of).reshape((-1,) + (1,) * (len(extent) - 1 - axis_at))
    return gain


def bell_draw(key, dims, scale, limit, shards=(), kind=jnp.bfloat16):
    loudness = block_levels(key, dims, shards, -0.22, 0.18) if shards else 1.0
    values = jax.random.normal(key, dims, jnp.float32) * scale * loudness
    return jnp.minimum(jnp.maximum(values, -limit), limit).astype(kind)


def setup_inputs(seed: int = 0) -> dict:
    key_list = jax.random.split(jax.random.key(seed), 5)
    return {
        "rhs": bell_draw(key_list[0], (LEVELS, SUPS, LOADS, BLOCK), 1.0, 6.0, ((0, 8), (1, 32)), jnp.float32),
        "inverse": draw_inverse(jax.random.fold_in(key_list[4], 71), 0),
        "factor": bell_draw(key_list[2], (LEVELS, SUPS, NB, BLOCK, BLOCK), (BLOCK * NB) ** -0.5, 0.1875, ((0, 8), (1, 32)), jnp.float32),
        "pattern": draw_pattern(jax.random.fold_in(key_list[4], 71), 0),
    }


def reference(rhs, inverse, factor, pattern):
    highest = lax.Precision.HIGHEST
    onehot = (pattern[..., None] == jnp.arange(SUPS, dtype=jnp.int32)).astype(jnp.float32)
    incoming = jnp.zeros((SUPS, LOADS, BLOCK), jnp.float32)
    forward_list = []
    for level in range(LEVELS):
        solved = jnp.einsum("jrb,jab->jra", rhs[level] - incoming, inverse[level], precision=highest)
        forward_list.append(solved)
        terms = jnp.einsum("jrb,jkab->jkra", solved, factor[level], precision=highest)
        incoming = jnp.einsum("jkc,jkra->cra", onehot[level], terms, precision=highest)
    outgoing = jnp.zeros((SUPS, LOADS, BLOCK), jnp.float32)
    solution_list = [None] * LEVELS
    for level in reversed(range(LEVELS)):
        solved = jnp.einsum("jra,jab->jrb", forward_list[level] - outgoing, inverse[level], precision=highest)
        solution_list[level] = solved
        if level > 0:
            picked = jnp.einsum("jkc,cra->jkra", onehot[level - 1], solved, precision=highest)
            outgoing = jnp.einsum("jkra,jkab->jrb", picked, factor[level - 1], precision=highest)
    return jnp.stack(forward_list), jnp.stack(solution_list)
```

```python
import functools

import jax
import jax.numpy as jnp
from jax import lax
from jax.experimental import pallas as pl
from jax.experimental.pallas import tpu as pltpu
from jax.sharding import Mesh
from jax.sharding import PartitionSpec as P

LEVELS, YH, YL, Z = 8, 2, 2, 8
GROUP = YL * Z
SUPS = YH * GROUP
NB, BLOCK, LOADS = 8, 128, 64
ROWS = LOADS // GROUP
AXES = ("chain", "yh", "yl", "z")
MEMBERS = ("yl", "z")
F32, BF16 = jnp.float32, jnp.bfloat16
VMEM = pl.BlockSpec(memory_space=pltpu.VMEM)
SMEM = pl.BlockSpec(memory_space=pltpu.SMEM)
PARAMS = pltpu.CompilerParams(vmem_limit_bytes=20 << 20)
PIECE = jax.ShapeDtypeStruct((GROUP, ROWS, BLOCK), F32)


def split(value):
    high = value.astype(BF16)
    return high, (value - high.astype(F32)).astype(BF16)


def split_kernel(source, high, low):
    high[...], low[...] = split(source[...])


def split_weights(weights):
    shape = jax.ShapeDtypeStruct((GROUP, BLOCK, NB * BLOCK), BF16)
    spec = pl.BlockSpec((2, BLOCK, NB * BLOCK), lambda i: (i, 0, 0))
    return pl.pallas_call(
        split_kernel, grid=(GROUP // 2,), in_specs=[spec], out_specs=[spec, spec], out_shape=[shape, shape], name="split_weights"
    )(weights)


def forward_kernel(step, arrivals, table, residue, *refs):
    arrived, (high, low, residue_out, own, other, total) = refs[:arrivals], refs[arrivals:]
    current = residue[...]
    for piece in arrived:
        current = current - piece[...]
    residue_out[...] = current

    @pl.when(table[GROUP, 0] == step)
    def _():
        total[...] = jnp.zeros_like(total)
        for sup in range(GROUP):
            left = jnp.concatenate(split(residue_out[sup]), axis=0)
            terms = jnp.dot(left, high[sup], preferred_element_type=F32) + jnp.dot(left, low[sup], preferred_element_type=F32)
            for k in range(NB):
                total[table[sup, k]] += terms[:, k * BLOCK : (k + 1) * BLOCK]
        summed = total[:, :ROWS] + total[:, ROWS:]
        own[...] = summed[:GROUP]
        other[...] = summed[GROUP:]


def forward_step(step, table, residue, arrived, high, low):
    return pl.pallas_call(
        functools.partial(forward_kernel, step, len(arrived)),
        in_specs=[SMEM] + [VMEM] * (3 + len(arrived)),
        out_specs=[VMEM] * 3,
        out_shape=[PIECE] * 3,
        scratch_shapes=[pltpu.VMEM((SUPS, 2 * ROWS, BLOCK), F32)],
        compiler_params=PARAMS,
        name=f"forward_{step}",
    )(table, residue, *arrived, high, low)


def backward_kernel(level, table, before, base, own, other, high, low, answer, picked):
    @pl.when(table[GROUP, 0] != level)
    def _():
        answer[...] = before[...]

    @pl.when(table[GROUP, 0] == level)
    def _():
        for half, source in enumerate((own, other)):
            value = source[...]
            top = value.astype(BF16).astype(F32)
            picked[half * GROUP : (half + 1) * GROUP, :ROWS] = top
            picked[half * GROUP : (half + 1) * GROUP, ROWS:] = value - top
        contract = (((1,), (1,)), ((), ()))
        for sup in range(GROUP):
            left = jnp.concatenate([picked[table[sup, k]] for k in range(NB)], axis=1).astype(BF16)
            terms = lax.dot_general(left, high[sup], contract, preferred_element_type=F32)
            terms += lax.dot_general(left, low[sup], contract, preferred_element_type=F32)
            answer[sup] = base[sup] - (terms[:ROWS] + terms[ROWS:])


def backward_step(level, table, before, base, own, other, high, low):
    return pl.pallas_call(
        functools.partial(backward_kernel, level),
        in_specs=[SMEM] + [VMEM] * 6,
        out_specs=VMEM,
        out_shape=PIECE,
        scratch_shapes=[pltpu.VMEM((SUPS, 2 * ROWS, BLOCK), F32)],
        compiler_params=PARAMS,
        name=f"backward_{level}",
    )(table, before, base, own, other, high, low)


def diagonal_kernel(residue, inverse, solved, base):
    highest = lax.Precision.HIGHEST
    for sup in range(GROUP):
        value = lax.dot_general(residue[sup], inverse[sup], (((1,), (1,)), ((), ())), precision=highest, preferred_element_type=F32)
        solved[sup] = value
        base[sup] = jnp.dot(value, inverse[sup], precision=highest, preferred_element_type=F32)


def diagonal(residue, inverse):
    return pl.pallas_call(
        diagonal_kernel, in_specs=[VMEM] * 2, out_specs=[VMEM] * 2, out_shape=[PIECE] * 2, compiler_params=PARAMS, name="diagonal"
    )(residue, inverse)


def index(chain, yh, yl, z):
    return ((chain * YH + yh) * YL + yl) * Z + z


def hop(value, source, target, cross):
    pairs = [
        (index(source, yh, yl, z), index(target, yh ^ cross, yl ^ cross, z)) for yh in range(YH) for yl in range(YL) for z in range(Z)
    ]
    return lax.ppermute(value, AXES, pairs)


def body(rhs, inverse, factor, pattern):
    highest = lax.Precision.HIGHEST
    place, side = lax.axis_index("chain"), lax.axis_index("yh")
    member = lax.axis_index("yl") * Z + lax.axis_index("z")
    last = place == LEVELS - 1
    diag, blocks = inverse[0, 0], factor[0, 0]

    with jax.named_scope("prepare"):
        square = jnp.einsum("ca,cb->ab", diag, diag, precision=highest)
        folded = jnp.einsum("kac,cb->bka", blocks, diag, precision=highest)
        closing = jnp.zeros((BLOCK, NB, BLOCK), F32).at[:, 0, :].set(square)
        own_weights = jnp.where(last, closing, folded).reshape(BLOCK, NB * BLOCK)
        own_targets = jnp.where(last, side * GROUP + member, pattern[0, 0]) ^ (side * GROUP)

    with jax.named_scope("gather"):
        weights = lax.all_gather(own_weights, MEMBERS, axis=0)
        targets = lax.all_gather(own_targets, MEMBERS, axis=0)
        diags = lax.all_gather(diag, MEMBERS, axis=0)
        table = jnp.concatenate([targets, jnp.full((1, NB), place, jnp.int32)], axis=0)

    def swapped(value):
        return jnp.where(side == 1, jnp.roll(value, LOADS // 2, axis=0), value)

    with jax.named_scope("spread_rhs"):
        residue = lax.all_to_all(swapped(rhs[0, 0]).reshape(GROUP, ROWS, BLOCK), MEMBERS, 0, 0)

    high, low = split_weights(weights)

    arrived = ()
    for step in range(LEVELS):
        residue, own, other = forward_step(step, table, residue, arrived, high, low)
        if step < LEVELS - 1:
            arrived = (hop(own, step, step + 1, 0), hop(other, step, step + 1, 1))

    solved, base = diagonal(residue, diags)
    answer = own
    for level in range(LEVELS - 2, -1, -1):
        arrived = (hop(answer, level + 1, level, 0), hop(answer, level + 1, level, 1))
        answer = backward_step(level, table, answer, base, *arrived, high, low)

    with jax.named_scope("collect"):
        both = jnp.concatenate([solved, answer], axis=1)
        home = lax.all_to_all(both, MEMBERS, 0, 0)
        outputs = [swapped(home[:, i * ROWS : (i + 1) * ROWS].reshape(LOADS, BLOCK)) for i in range(2)]
    return outputs[0][None, None], outputs[1][None, None]


def solution(mesh):
    fine = Mesh(mesh.devices.reshape(LEVELS, YH, YL, Z), AXES)
    column = ("yh", "yl", "z")
    specs = [P("chain", column, *([None] * rank)) for rank in (2, 2, 3, 1)]
    return jax.shard_map(body, mesh=fine, in_specs=tuple(specs), out_specs=(specs[0], specs[0]), check_vma=False)
```

```python
import functools

import jax
import jax.numpy as jnp
from jax import lax
from jax.experimental import pallas as pl
from jax.experimental.pallas import tpu as pltpu
from jax.sharding import Mesh
from jax.sharding import PartitionSpec as P

LEVELS, Y, Z = 8, 4, 8
CLASS = 2 * Z
NB, BLOCK, LOADS = 8, 128, 64
ROWS = LOADS // Z
WIDE = NB * BLOCK
AXES = ("chain", "y", "z")
F32, BF16, I32 = jnp.float32, jnp.bfloat16, jnp.int32
VMEM = pl.BlockSpec(memory_space=pltpu.VMEM)
SMEM = pl.BlockSpec(memory_space=pltpu.SMEM)
PARAMS = pltpu.CompilerParams(vmem_limit_bytes=24 << 20)
PIECE = jax.ShapeDtypeStruct((CLASS, ROWS, BLOCK), F32)
GROUPS = (
    ((0, 0), (0, 1), (-1, 0), (1, 0), (-1, 1), (1, 1)),
    ((-2, 0), (2, 0), (-2, 1), (2, 1)),
    ((-3, 0), (3, 0), (-3, 1), (3, 1), (-4, 0), (4, 1)),
)


def split(value):
    high = value.astype(BF16)
    return high, (value - high.astype(F32)).astype(BF16)


def split_kernel(count, *refs):
    high, low = refs[count:]
    for i, source in enumerate(refs[:count]):
        high[i], low[i] = split(source[...])


def split_weights(pieces):
    shape = jax.ShapeDtypeStruct((len(pieces), BLOCK, WIDE + BLOCK), BF16)
    return pl.pallas_call(
        functools.partial(split_kernel, len(pieces)),
        in_specs=[VMEM] * len(pieces),
        out_specs=[VMEM] * 2,
        out_shape=[shape] * 2,
        compiler_params=PARAMS,
        name="split_weights",
    )(*pieces)


def supernodes(table, weights):
    for group, (high, low) in zip(GROUPS, zip(weights[::2], weights[1::2])):
        for i, (away, slot) in enumerate(group):
            yield lax.rem(table[CLASS, 1] + (Z + away), Z) * 2 + slot, high.at[i], low.at[i]


def forward_kernel(step, arrivals, table, residue, *refs):
    arrived, weights, (residue_out, own, other, total) = refs[:arrivals], refs[arrivals:-4], refs[-4:]
    current = residue[...]
    for piece in arrived:
        current = current - piece[...]
    residue_out[...] = current

    @pl.when(table[CLASS, 0] == step)
    def _():
        total[...] = jnp.zeros_like(total)
        for sup, high, low in supernodes(table, weights):
            left = jnp.concatenate(split(residue_out[sup]), axis=0)
            terms = jnp.dot(left, high[:, :WIDE], preferred_element_type=F32) + jnp.dot(left, low[:, :WIDE], preferred_element_type=F32)
            summed = terms[:ROWS] + terms[ROWS:]
            for k in range(NB):
                total[table[sup, k]] += summed[:, k * BLOCK : (k + 1) * BLOCK]
        own[...] = total[:CLASS]
        other[...] = total[CLASS:]


def forward_step(step, table, residue, arrived, weights):
    return pl.pallas_call(
        functools.partial(forward_kernel, step, len(arrived)),
        in_specs=[SMEM] + [VMEM] * (1 + len(arrived) + len(weights)),
        out_specs=[VMEM] * 3,
        out_shape=[PIECE] * 3,
        scratch_shapes=[pltpu.VMEM((2 * CLASS, ROWS, BLOCK), F32)],
        compiler_params=PARAMS,
        name=f"forward_{step}",
    )(table, residue, *arrived, *weights)


CONTRACT_LAST = (((1,), (1,)), ((), ()))


def backward_kernel(level, table, before, base, own, other, *refs):
    weights, (answer, picked) = refs[:-2], refs[-2:]

    @pl.when(table[CLASS, 0] != level)
    def _():
        answer[...] = before[...]

    @pl.when(table[CLASS, 0] == level)
    def _():
        for half, source in enumerate((own, other)):
            value = source[...]
            top = value.astype(BF16).astype(F32)
            picked[half * CLASS : (half + 1) * CLASS, :ROWS] = top
            picked[half * CLASS : (half + 1) * CLASS, ROWS:] = value - top
        for sup, high, low in supernodes(table, weights):
            left = jnp.concatenate([picked[table[sup, k]] for k in range(NB)], axis=1).astype(BF16)
            terms = lax.dot_general(left, high[:, :WIDE], CONTRACT_LAST, preferred_element_type=F32)
            terms += lax.dot_general(left, low[:, :WIDE], CONTRACT_LAST, preferred_element_type=F32)
            answer[sup] = base[sup] - (terms[:ROWS] + terms[ROWS:])


def backward_step(level, table, before, base, own, other, weights):
    return pl.pallas_call(
        functools.partial(backward_kernel, level),
        in_specs=[SMEM] + [VMEM] * (4 + len(weights)),
        out_specs=VMEM,
        out_shape=PIECE,
        scratch_shapes=[pltpu.VMEM((2 * CLASS, 2 * ROWS, BLOCK), F32)],
        compiler_params=PARAMS,
        name=f"backward_{level}",
    )(table, before, base, own, other, *weights)


def diagonal_kernel(table, residue, *refs):
    weights, (solved, base) = refs[:-2], refs[-2:]
    for sup, high, low in supernodes(table, weights):
        left = jnp.concatenate(split(residue[sup]), axis=0)
        terms = jnp.dot(left, high[:, WIDE:], preferred_element_type=F32) + jnp.dot(left, low[:, WIDE:], preferred_element_type=F32)
        value = terms[:ROWS] + terms[ROWS:]
        solved[sup] = value
        left = jnp.concatenate(split(value), axis=0)
        terms = lax.dot_general(left, high[:, WIDE:], CONTRACT_LAST, preferred_element_type=F32)
        terms += lax.dot_general(left, low[:, WIDE:], CONTRACT_LAST, preferred_element_type=F32)
        base[sup] = terms[:ROWS] + terms[ROWS:]


def diagonal(table, residue, weights):
    return pl.pallas_call(
        diagonal_kernel,
        in_specs=[SMEM] + [VMEM] * (1 + len(weights)),
        out_specs=[VMEM] * 2,
        out_shape=[PIECE] * 2,
        compiler_params=PARAMS,
        name="diagonal",
    )(table, residue, *weights)


def index(chain, y, z):
    return (chain * Y + y) * Z + z


def seat(level, side):
    return side if level % 2 == 0 else Y - 1 - side


def hop(value, source, target, cross):
    pairs = [(index(source, seat(source, side), z), index(target, seat(target, side ^ cross), z)) for side in range(2) for z in range(Z)]
    return lax.ppermute(value, AXES, pairs)


def ring(value, steps):
    pairs = [
        (index(level, seat(level, side), z), index(level, seat(level, side), (z + steps) % Z))
        for level in range(LEVELS)
        for side in range(2)
        for z in range(Z)
    ]
    return lax.ppermute(value, AXES, pairs)


def seated(value, back=False):
    pairs = [
        (index(level, Y - 1 - seat(level, side), z), index(level, seat(level, side), z))
        for level in range(LEVELS)
        for side in range(2)
        for z in range(Z)
    ]
    return lax.ppermute(value, AXES, [pair[::-1] for pair in pairs] if back else pairs)


def body(rhs, inverse, factor, pattern):
    highest = lax.Precision.HIGHEST
    place, row, member = lax.axis_index("chain"), lax.axis_index("y"), lax.axis_index("z")
    last = place == LEVELS - 1
    odd = place % 2
    active = (row >= Y // 2) == (odd == 1)
    side = ((row == 1) | (row == 2)).astype(I32)
    diag, blocks = inverse[0, 0], factor[0, 0]

    with jax.named_scope("prepare"):
        square = jnp.einsum("ca,cb->ab", diag, diag, precision=highest)
        folded = jnp.einsum("kac,cb->bka", blocks, diag, precision=highest)
        closing = jnp.zeros((BLOCK, NB, BLOCK), F32).at[:, 0, :].set(square)
        weight_a = jnp.concatenate([jnp.where(last, closing, folded).reshape(BLOCK, WIDE), diag.T], axis=1)
        there, along = pattern[0, 0] // Z, pattern[0, 0] % Z
        there_side = ((there == 1) | (there == 2)).astype(I32)
        there_slot = ((there >= Y // 2) == (odd == 1)).astype(I32)
        targets = (there_side ^ side) * CLASS + along * 2 + there_slot
        targets = jnp.where(last, member * 2 + 1 - active.astype(I32), targets)
        small_a = jnp.concatenate([rhs[0, 0], jnp.zeros((8, BLOCK), F32).at[0, :NB].set(targets.astype(F32))], axis=0)

    with jax.named_scope("gather"):
        weight_b = seated(weight_a)
        small_b = seated(small_a)
        left_a, right_a = ring(weight_a, 1), ring(weight_a, -1)
        left_b, right_b = ring(weight_b, 1), ring(weight_b, -1)
        pieces = [[weight_a, weight_b, left_a, right_a, left_b, right_b]]
        for _ in range(2):
            left_a, right_a = ring(left_a, 1), ring(right_a, -1)
            left_b, right_b = ring(left_b, 1), ring(right_b, -1)
            pieces.append([left_a, right_a, left_b, right_b])
        pieces[2] += [ring(left_a, 1), ring(right_b, -1)]
        weights = [part for group in pieces for part in split_weights(group)]

    with jax.named_scope("spread_rhs"):
        marks = jnp.concatenate([small_a[LOADS : LOADS + 1], small_b[LOADS : LOADS + 1], jnp.zeros((6, BLOCK), F32)], axis=0)
        parts = [small_a[:LOADS].reshape(Z, ROWS, BLOCK), small_b[:LOADS].reshape(Z, ROWS, BLOCK), jnp.broadcast_to(marks, (Z, 8, BLOCK))]
        mine = lax.all_to_all(jnp.concatenate(parts, axis=1), "z", 0, 0)
        residue = mine[:, : 2 * ROWS].reshape(CLASS, ROWS, BLOCK)
        table = mine[:, 2 * ROWS : 2 * ROWS + 2, :NB].reshape(CLASS, NB).astype(I32)
        final = jnp.zeros((1, NB), I32).at[0, 0].set(jnp.where(active, place, -1)).at[0, 1].set(member)
        table = jnp.concatenate([table, final], axis=0)

    arrived = ()
    for step in range(LEVELS):
        residue, own, other = forward_step(step, table, residue, arrived, weights)
        if step < LEVELS - 1:
            arrived = (hop(other, step, step + 1, 1), hop(own, step, step + 1, 0))

    solved, base = diagonal(table, residue, weights)
    answer = own
    for level in range(LEVELS - 2, -1, -1):
        other = hop(answer, level + 1, level, 1)
        own = hop(answer, level + 1, level, 0)
        answer = backward_step(level, table, answer, base, own, other, weights)

    with jax.named_scope("collect"):
        both = jnp.concatenate([solved.reshape(Z, 2 * ROWS, BLOCK), answer.reshape(Z, 2 * ROWS, BLOCK)], axis=1)
        home = lax.all_to_all(both, "z", 0, 0).reshape(Z, 2, 2, ROWS, BLOCK).transpose(2, 1, 0, 3, 4).reshape(2, 2, LOADS, BLOCK)
        result = jnp.where(active, home[0], seated(home[1], back=True))
    return result[0][None, None], result[1][None, None]


def solution(mesh):
    fine = Mesh(mesh.devices.reshape(LEVELS, Y, Z), AXES)
    column = ("y", "z")
    specs = [P("chain", column, *([None] * rank)) for rank in (2, 2, 3, 1)]
    return jax.shard_map(body, mesh=fine, in_specs=tuple(specs), out_specs=(specs[0], specs[0]), check_vma=False)
```

```python
import functools

import jax
import jax.numpy as jnp
from jax import lax
from jax.experimental import pallas as pl
from jax.experimental.pallas import tpu as pltpu
from jax.sharding import Mesh
from jax.sharding import PartitionSpec as P

LEVELS, Y, Z = 8, 4, 8
CLASS = 2 * Z
NB, BLOCK, LOADS = 8, 128, 64
ROWS = LOADS // Z
WIDE = NB * BLOCK
AXES = ("chain", "y", "z")
TEAMS = [[y * Z + z for y in (side, Y - 1 - side) for z in range(Z)] for side in range(2)]
F32, BF16, I32 = jnp.float32, jnp.bfloat16, jnp.int32
VMEM = pl.BlockSpec(memory_space=pltpu.VMEM)
SMEM = pl.BlockSpec(memory_space=pltpu.SMEM)
ANY = pl.BlockSpec(memory_space=pl.ANY)
PARAMS = pltpu.CompilerParams(vmem_limit_bytes=24 << 20)
PIECE = jax.ShapeDtypeStruct((CLASS, ROWS, BLOCK), F32)
PACKED = jax.ShapeDtypeStruct((BLOCK, WIDE + BLOCK), F32)
GROUPS = (
    ((0, 0), (0, 1), (-1, 0), (1, 0), (-1, 1), (1, 1)),
    ((-2, 0), (2, 0), (-2, 1), (2, 1)),
    ((-3, 0), (3, 0), (-3, 1), (3, 1), (-4, 0), (4, 1)),
)
HIGHEST = lax.Precision.HIGHEST
CONTRACT_LAST = (((1,), (1,)), ((), ()))


def half_of(row):
    return (row >= Y // 2).astype(I32) if hasattr(row, "astype") else int(row >= Y // 2)


def side_of(row):
    return ((row == 1) | (row == 2)).astype(I32)


def prepare_kernel(pattern, rhs, inverse, factor, weights, spread):
    place, row, member = lax.axis_index("chain"), lax.axis_index("y"), lax.axis_index("z")
    last = place == LEVELS - 1
    side = side_of(row)
    turned = inverse[...].T
    weights[:, WIDE:] = turned

    @pl.when(last)
    def _():
        weights[:, :BLOCK] = jnp.dot(turned, inverse[...], precision=HIGHEST, preferred_element_type=F32)
        weights[:, BLOCK:WIDE] = jnp.zeros((BLOCK, WIDE - BLOCK), F32)

    @pl.when(jnp.logical_not(last))
    def _():
        for k in range(NB):
            weights[:, k * BLOCK : (k + 1) * BLOCK] = lax.dot_general(
                turned, factor[k], CONTRACT_LAST, precision=HIGHEST, preferred_element_type=F32
            )

    lane = lax.broadcasted_iota(I32, (8, BLOCK), 1)
    marks = jnp.zeros((8, BLOCK), F32)
    for k in range(NB):
        target = pattern[0, k]
        there = lax.div(target, Z)
        number = (side_of(there) ^ side) * CLASS + half_of(there) * Z + lax.rem(target, Z)
        number = jnp.where(last, half_of(row) * Z + member, number)
        marks = jnp.where(lane == k, number.astype(F32), marks)
    for i in range(CLASS):
        spread[i, :ROWS] = rhs[(i % Z) * ROWS : (i % Z + 1) * ROWS]
        spread[i, ROWS:] = marks


def prepare(pattern, rhs, inverse, factor):
    return pl.pallas_call(
        prepare_kernel,
        in_specs=[SMEM] + [VMEM] * 3,
        out_specs=[VMEM] * 2,
        out_shape=[PACKED, jax.ShapeDtypeStruct((CLASS, 2 * ROWS, BLOCK), F32)],
        compiler_params=PARAMS,
        name="prepare",
    )(pattern, rhs, inverse, factor)


def receive_kernel(mine, passed, residue, table, passed_out):
    residue[...] = mine[:, :ROWS]
    table[...] = mine[:, ROWS].astype(I32)


def receive(mine, passed):
    return pl.pallas_call(
        receive_kernel,
        in_specs=[VMEM, ANY],
        out_specs=[VMEM, VMEM, ANY],
        out_shape=[PIECE, jax.ShapeDtypeStruct((CLASS, BLOCK), I32), PACKED],
        input_output_aliases={1: 2},
        compiler_params=PARAMS,
        name="receive",
    )(mine, passed)


def split(value):
    high = value.astype(BF16)
    return high, (value - high.astype(F32)).astype(BF16)


def split_kernel(count, *refs):
    high, low = refs[count:]
    for i, source in enumerate(refs[:count]):
        high[i], low[i] = split(source[...])


def split_weights(pieces):
    shape = jax.ShapeDtypeStruct((len(pieces), BLOCK, WIDE + BLOCK), BF16)
    return pl.pallas_call(
        functools.partial(split_kernel, len(pieces)),
        in_specs=[VMEM] * len(pieces),
        out_specs=[VMEM] * 2,
        out_shape=[shape] * 2,
        compiler_params=PARAMS,
        cost_estimate=pl.CostEstimate(flops=0, transcendentals=0, bytes_accessed=8 * len(pieces) * BLOCK * (WIDE + BLOCK)),
        name="split_weights",
    )(*pieces)


def supernodes(weights):
    member, odd = lax.axis_index("z"), lax.rem(lax.axis_index("chain"), 2)
    for group, (high, low) in zip(GROUPS, zip(weights[::2], weights[1::2])):
        for i, (away, other) in enumerate(group):
            yield (odd ^ other) * Z + lax.rem(member + (Z + away), Z), high.at[i], low.at[i]


def active(level):
    return (lax.axis_index("chain") == level) & (half_of(lax.axis_index("y")) == level % 2)


def forward_kernel(step, arrivals, table, residue, *refs):
    arrived, weights, (residue_out, own, other, total) = refs[:arrivals], refs[arrivals:-4], refs[-4:]

    @pl.when(jnp.logical_not(active(step)))
    def _():
        residue_out[...] = residue[...]

    @pl.when(active(step))
    def _():
        current = residue[...]
        for piece in arrived:
            current = current - piece[...]
        residue_out[...] = current
        total[...] = jnp.zeros_like(total)
        for sup, high, low in supernodes(weights):
            left = jnp.concatenate(split(residue_out[sup]), axis=0)
            terms = jnp.dot(left, high[:, :WIDE], preferred_element_type=F32) + jnp.dot(left, low[:, :WIDE], preferred_element_type=F32)
            summed = terms[:ROWS] + terms[ROWS:]
            for k in range(NB):
                total[table[sup, k]] += summed[:, k * BLOCK : (k + 1) * BLOCK]
        own[...] = total[:CLASS]
        other[...] = total[CLASS:]


def forward_step(step, table, residue, arrived, weights):
    return pl.pallas_call(
        functools.partial(forward_kernel, step, len(arrived)),
        in_specs=[SMEM] + [VMEM] * (1 + len(arrived) + len(weights)),
        out_specs=[VMEM] * 3,
        out_shape=[PIECE] * 3,
        scratch_shapes=[pltpu.VMEM((2 * CLASS, ROWS, BLOCK), F32)],
        compiler_params=PARAMS,
        name=f"forward_{step}",
    )(table, residue, *arrived, *weights)


def backward_kernel(level, table, before, base, own, other, *refs):
    weights, (answer, picked) = refs[:-2], refs[-2:]

    @pl.when(jnp.logical_not(active(level)))
    def _():
        answer[...] = before[...]

    @pl.when(active(level))
    def _():
        for half, source in enumerate((own, other)):
            picked[half * CLASS : (half + 1) * CLASS] = jnp.concatenate(split(source[...]), axis=1)
        for sup, high, low in supernodes(weights):
            left = jnp.concatenate([picked[table[sup, k]] for k in range(NB)], axis=1)
            terms = lax.dot_general(left, high[:, :WIDE], CONTRACT_LAST, preferred_element_type=F32)
            terms += lax.dot_general(left, low[:, :WIDE], CONTRACT_LAST, preferred_element_type=F32)
            answer[sup] = base[sup] - (terms[:ROWS] + terms[ROWS:])


def backward_step(level, table, before, base, own, other, weights):
    return pl.pallas_call(
        functools.partial(backward_kernel, level),
        in_specs=[SMEM] + [VMEM] * (4 + len(weights)),
        out_specs=VMEM,
        out_shape=PIECE,
        scratch_shapes=[pltpu.VMEM((2 * CLASS, 2 * ROWS, BLOCK), BF16)],
        compiler_params=PARAMS,
        name=f"backward_{level}",
    )(table, before, base, own, other, *weights)


def diagonal_kernel(residue, *refs):
    weights, (solved, base) = refs[:-2], refs[-2:]
    for sup, high, low in supernodes(weights):
        left = jnp.concatenate(split(residue[sup]), axis=0)
        terms = jnp.dot(left, high[:, WIDE:], preferred_element_type=F32) + jnp.dot(left, low[:, WIDE:], preferred_element_type=F32)
        value = terms[:ROWS] + terms[ROWS:]
        solved[sup] = value
        left = jnp.concatenate(split(value), axis=0)
        terms = lax.dot_general(left, high[:, WIDE:], CONTRACT_LAST, preferred_element_type=F32)
        terms += lax.dot_general(left, low[:, WIDE:], CONTRACT_LAST, preferred_element_type=F32)
        base[sup] = terms[:ROWS] + terms[ROWS:]


def diagonal(residue, weights):
    return pl.pallas_call(
        diagonal_kernel,
        in_specs=[VMEM] * (1 + len(weights)),
        out_specs=[VMEM] * 2,
        out_shape=[PIECE] * 2,
        compiler_params=PARAMS,
        name="diagonal",
    )(residue, *weights)


def index(chain, y, z):
    return (chain * Y + y) * Z + z


def seat(level, side):
    return side if level % 2 == 0 else Y - 1 - side


def hop(value, source, target, cross):
    both = [(first, first + target - source) for first in (source % 4, source % 4 + 4)]
    pairs = [
        (index(first, seat(first, side), z), index(second, seat(second, side ^ cross), z))
        for first, second in both
        if 0 <= second < LEVELS
        for side in range(2)
        for z in range(Z)
    ]
    return lax.ppermute(value, AXES, pairs)


def ring(value, steps, native=False):
    pairs = []
    for level in range(LEVELS):
        for side in range(2):
            row = seat(level, side)
            source = Y - 1 - row if native else row
            pairs += [(index(level, source, z), index(level, row, (z + steps) % Z)) for z in range(Z)]
    return lax.ppermute(value, AXES, pairs)


def exchange(value):
    return lax.all_to_all(value, ("y", "z"), 0, 0, axis_index_groups=TEAMS)


def body(rhs, inverse, factor, pattern):
    weight_a, spread = prepare(pattern[0], rhs[0, 0], inverse[0, 0], factor[0, 0])

    with jax.named_scope("gather"):
        left_a, right_a = ring(weight_a, 1), ring(weight_a, -1)
        weight_b, left_b, right_b = ring(weight_a, 0, True), ring(weight_a, 1, True), ring(weight_a, -1, True)
        residue, table, left_a = receive(exchange(spread), left_a)
        table = table[:, :NB]
        pieces = [[weight_a, weight_b, left_a, right_a, left_b, right_b]]
        for _ in range(2):
            left_a, right_a = ring(left_a, 1), ring(right_a, -1)
            left_b, right_b = ring(left_b, 1), ring(right_b, -1)
            pieces.append([left_a, right_a, left_b, right_b])
        pieces[2] += [ring(left_a, 1), ring(right_b, -1)]
        weights = [part for group in pieces for part in split_weights(group)]

    arrived = ()
    for step in range(LEVELS):
        residue, own, other = forward_step(step, table, residue, arrived, weights)
        if step < LEVELS - 1:
            arrived = (hop(other, step, step + 1, 1), hop(own, step, step + 1, 0))

    solved, base = diagonal(residue, weights)
    answer = own
    for level in range(LEVELS - 2, -1, -1):
        other = hop(answer, level + 1, level, 1)
        own = hop(answer, level + 1, level, 0)
        answer = backward_step(level, table, answer, base, own, other, weights)

    with jax.named_scope("collect"):
        home = exchange(jnp.concatenate([solved, answer], axis=1))
        home = jnp.where(lax.axis_index("chain") % 2 == 1, home[Z:], home[:Z])
    return home[:, :ROWS].reshape(1, 1, LOADS, BLOCK), home[:, ROWS:].reshape(1, 1, LOADS, BLOCK)


def solution(mesh):
    fine = Mesh(mesh.devices.reshape(LEVELS, Y, Z), AXES)
    column = ("y", "z")
    specs = [P("chain", column, *([None] * rank)) for rank in (2, 2, 3, 1)]
    return jax.shard_map(body, mesh=fine, in_specs=tuple(specs), out_specs=(specs[0], specs[0]), check_vma=False)
```

```python
import functools

import jax
import jax.numpy as jnp
from jax import lax
from jax.experimental import pallas as pl
from jax.experimental.pallas import tpu as pltpu
from jax.sharding import Mesh
from jax.sharding import PartitionSpec as P

LEVELS, Y, Z = 8, 4, 8
CLASS = 2 * Z
NB, BLOCK, LOADS = 8, 128, 64
ROWS = LOADS // Z
WIDE = NB * BLOCK
AXES = ("chain", "y", "z")
TEAMS = [[y * Z + z for y in (side, Y - 1 - side) for z in range(Z)] for side in range(2)]
F32, BF16, I32 = jnp.float32, jnp.bfloat16, jnp.int32
VMEM = pl.BlockSpec(memory_space=pltpu.VMEM)
SMEM = pl.BlockSpec(memory_space=pltpu.SMEM)
HBM = pl.BlockSpec(memory_space=pltpu.HBM)
PARAMS = pltpu.CompilerParams(vmem_limit_bytes=24 << 20)
PIECE = jax.ShapeDtypeStruct((CLASS, ROWS, BLOCK), F32)
PACKED = jax.ShapeDtypeStruct((BLOCK + ROWS, WIDE + BLOCK), F32)
GROUPS = (
    ((0, 0), (0, 1), (-1, 0), (1, 0), (-1, 1), (1, 1)),
    ((-2, 0), (2, 0), (-2, 1), (2, 1)),
    ((-3, 0), (3, 0), (-3, 1), (3, 1), (-4, 0), (4, 1)),
)
HIGHEST = lax.Precision.HIGHEST
CONTRACT_LAST = (((1,), (1,)), ((), ()))


def half_at(level):
    return (level + level // 2) % 2


def half_of(row):
    return (row >= Y // 2).astype(I32) if hasattr(row, "astype") else int(row >= Y // 2)


def side_of(row):
    return ((row == 1) | (row == 2)).astype(I32)


def prepare_kernel(pattern_far, rhs_far, inverse_far, factor_far, piece, pattern, rhs, inverse, factor, arrival):
    copies = [
        pltpu.make_async_copy(source, target, arrival.at[i])
        for i, (source, target) in enumerate(((inverse_far, inverse), (factor_far, factor), (rhs_far, rhs), (pattern_far, pattern)))
    ]
    for copy in copies:
        copy.start()
    place, row, member = lax.axis_index("chain"), lax.axis_index("y"), lax.axis_index("z")
    last = place == LEVELS - 1
    side = side_of(row)
    copies[0].wait()
    turned = inverse[...].T
    piece[:BLOCK, WIDE:] = turned
    copies[1].wait()

    @pl.when(last)
    def _():
        piece[:BLOCK, :BLOCK] = jnp.dot(turned, inverse[...], precision=HIGHEST, preferred_element_type=F32)
        piece[:BLOCK, BLOCK:WIDE] = jnp.zeros((BLOCK, WIDE - BLOCK), F32)

    @pl.when(jnp.logical_not(last))
    def _():
        for k in range(NB):
            piece[:BLOCK, k * BLOCK : (k + 1) * BLOCK] = lax.dot_general(
                turned, factor[k], CONTRACT_LAST, precision=HIGHEST, preferred_element_type=F32
            )

    copies[2].wait()
    copies[3].wait()
    lane = lax.broadcasted_iota(I32, (8, BLOCK), 1)
    marks = jnp.zeros((8, BLOCK), F32)
    for k in range(NB):
        target = pattern[0, k]
        there = lax.div(target, Z)
        seat_number = (side_of(there) ^ side) * CLASS + half_of(there) * Z + lax.rem(target, Z)
        seat_number = jnp.where(last, half_of(row) * Z + member, seat_number)
        marks = jnp.where(lane == k, seat_number.astype(F32), marks)
    piece[BLOCK:, WIDE:] = marks
    for i in range(Z):
        piece[BLOCK:, i * BLOCK : (i + 1) * BLOCK] = rhs[i * ROWS : (i + 1) * ROWS]


def prepare(pattern, rhs, inverse, factor):
    return pl.pallas_call(
        prepare_kernel,
        in_specs=[HBM] * 4,
        out_specs=VMEM,
        out_shape=PACKED,
        scratch_shapes=[
            pltpu.SMEM((1, NB), I32),
            pltpu.VMEM((LOADS, BLOCK), F32),
            pltpu.VMEM((BLOCK, BLOCK), F32),
            pltpu.VMEM((NB, BLOCK, BLOCK), F32),
            pltpu.SemaphoreType.DMA((4,)),
        ],
        compiler_params=PARAMS,
        name="prepare",
    )(pattern, rhs, inverse, factor)


def split(value):
    high = value.astype(BF16)
    return high, (value - high.astype(F32)).astype(BF16)


def split_kernel(count, *refs):
    high, low = refs[count:]
    for i, source in enumerate(refs[:count]):
        high[i], low[i] = split(source[:BLOCK, :WIDE])


def split_weights(pieces):
    shape = jax.ShapeDtypeStruct((len(pieces), BLOCK, WIDE), BF16)
    return pl.pallas_call(
        functools.partial(split_kernel, len(pieces)),
        in_specs=[VMEM] * len(pieces),
        out_specs=[VMEM] * 2,
        out_shape=[shape] * 2,
        compiler_params=PARAMS,
        cost_estimate=pl.CostEstimate(flops=0, transcendentals=0, bytes_accessed=8 * len(pieces) * BLOCK * WIDE),
        name="split_weights",
    )(*pieces)


def number(away, other):
    member = lax.axis_index("z")
    return (half_at(lax.axis_index("chain")) ^ other) * Z + lax.rem(member + (Z + away), Z)


ORDER = [step for group in GROUPS for step in group]


def receive_kernel(*refs):
    pieces, (residue, table) = refs[:-2], refs[-2:]
    mine = pl.ds(pl.multiple_of(lax.axis_index("z") * BLOCK, BLOCK), BLOCK)
    for step, piece in zip(ORDER, pieces):
        residue[number(*step)] = piece[BLOCK:, mine]
        table[number(*step)] = piece[BLOCK:, WIDE:].astype(I32)


def receive(pieces):
    return pl.pallas_call(
        receive_kernel,
        in_specs=[VMEM] * len(pieces),
        out_specs=[VMEM, VMEM],
        out_shape=[PIECE, jax.ShapeDtypeStruct(PIECE.shape, I32)],
        compiler_params=PARAMS,
        name="receive",
    )(*pieces)


def supernodes(weights):
    for group, (high, low) in zip(GROUPS, zip(weights[::2], weights[1::2])):
        for i, (away, other) in enumerate(group):
            yield number(away, other), high.at[i], low.at[i]


def active(level):
    return (lax.axis_index("chain") == level) & (half_of(lax.axis_index("y")) == half_at(level))


def forward_kernel(step, arrivals, table, residue, *refs):
    arrived, weights, (residue_out, own, other, total) = refs[:arrivals], refs[arrivals:-4], refs[-4:]

    @pl.when(jnp.logical_not(active(step)))
    def _():
        residue_out[...] = residue[...]

    @pl.when(active(step))
    def _():
        current = residue[...]
        for piece in arrived:
            current = current - piece[...]
        residue_out[...] = current
        if step < LEVELS - 1:
            total[...] = jnp.zeros_like(total)
        for sup, high, low in supernodes(weights):
            left = jnp.concatenate(split(residue_out[sup]), axis=0)
            if step == LEVELS - 1:
                terms = jnp.dot(left, high[:, :BLOCK], preferred_element_type=F32) + jnp.dot(left, low[:, :BLOCK], preferred_element_type=F32)
                own[sup] = terms[:ROWS] + terms[ROWS:]
                continue
            terms = jnp.dot(left, high[...], preferred_element_type=F32) + jnp.dot(left, low[...], preferred_element_type=F32)
            summed = terms[:ROWS] + terms[ROWS:]
            for k in range(NB):
                total[table[sup, k]] += summed[:, k * BLOCK : (k + 1) * BLOCK]
        if step < LEVELS - 1:
            own[...] = total[:CLASS]
            other[...] = total[CLASS:]


def forward_step(step, table, residue, arrived, weights):
    return pl.pallas_call(
        functools.partial(forward_kernel, step, len(arrived)),
        in_specs=[SMEM] + [VMEM] * (1 + len(arrived) + len(weights)),
        out_specs=[VMEM] * 3,
        out_shape=[PIECE] * 3,
        scratch_shapes=[pltpu.VMEM((2 * CLASS, ROWS, BLOCK), F32)],
        compiler_params=PARAMS,
        name=f"forward_{step}",
    )(table, residue, *arrived, *weights)


def turn_kernel(*refs):
    for source, target in zip(refs[:6], refs[6:]):
        for i in range(source.shape[0]):
            for k in range(NB):
                target[i, k * BLOCK : (k + 1) * BLOCK] = source[i, :, k * BLOCK : (k + 1) * BLOCK].T


def turn(weights):
    return pl.pallas_call(
        turn_kernel,
        in_specs=[VMEM] * len(weights),
        out_specs=[VMEM] * len(weights),
        out_shape=[jax.ShapeDtypeStruct((part.shape[0], WIDE, BLOCK), BF16) for part in weights],
        compiler_params=PARAMS,
        name="turn",
    )(*weights)


def backward_kernel(level, table, before, base, own, other, *refs):
    weights, (answer, picked) = refs[:-2], refs[-2:]

    @pl.when(jnp.logical_not(active(level)))
    def _():
        answer[...] = before[...]

    @pl.when(active(level))
    def _():
        for half, source in enumerate((own, other)):
            picked[half * CLASS : (half + 1) * CLASS] = jnp.concatenate(split(source[...]), axis=1)
        for sup, high, low in supernodes(weights):
            left = jnp.concatenate([picked[table[sup, k]] for k in range(NB)], axis=1)
            terms = jnp.dot(left, high[...], preferred_element_type=F32) + jnp.dot(left, low[...], preferred_element_type=F32)
            answer[sup] = base[sup] - (terms[:ROWS] + terms[ROWS:])


def backward_step(level, table, before, base, own, other, weights):
    return pl.pallas_call(
        functools.partial(backward_kernel, level),
        in_specs=[SMEM] + [VMEM] * (4 + len(weights)),
        out_specs=VMEM,
        out_shape=PIECE,
        scratch_shapes=[pltpu.VMEM((2 * CLASS, 2 * ROWS, BLOCK), BF16)],
        compiler_params=PARAMS,
        name=f"backward_{level}",
    )(table, before, base, own, other, *weights)


def double(left, right, dims):
    terms = 0.0
    for part in split(right):
        terms += lax.dot_general(jnp.concatenate(split(left), axis=0), part, dims, preferred_element_type=F32)
    return terms[:ROWS] + terms[ROWS:]


def diagonal_kernel(residue, *refs):
    pieces, (solved, base) = refs[:-2], refs[-2:]
    for step, piece in zip(ORDER, pieces):
        sup, turned = number(*step), piece[:BLOCK, WIDE:]
        value = double(residue[sup], turned, (((1,), (0,)), ((), ())))
        solved[sup] = value
        base[sup] = double(value, turned, CONTRACT_LAST)


def diagonal(residue, pieces):
    return pl.pallas_call(
        diagonal_kernel,
        in_specs=[VMEM] * (1 + len(pieces)),
        out_specs=[VMEM] * 2,
        out_shape=[PIECE] * 2,
        compiler_params=PARAMS,
        name="diagonal",
    )(residue, *pieces)


def index(chain, y, z):
    return (chain * Y + y) * Z + z


def seat(level, side):
    return side if half_at(level) == 0 else Y - 1 - side


def hop(value, source, target, cross):
    both = [(first, first + target - source) for first in (source % 4, source % 4 + 4)]
    pairs = [
        (index(first, seat(first, side), z), index(second, seat(second, side ^ cross), z))
        for first, second in both
        if 0 <= second < LEVELS
        for side in range(2)
        for z in range(Z)
    ]
    return lax.ppermute(value, AXES, pairs)


def ring(value, steps, native=False):
    pairs = []
    for level in range(LEVELS):
        for side in range(2):
            row = seat(level, side)
            source = Y - 1 - row if native else row
            pairs += [(index(level, source, z), index(level, row, (z + steps) % Z)) for z in range(Z)]
    return lax.ppermute(value, AXES, pairs)


def exchange(value):
    return lax.all_to_all(value, ("y", "z"), 0, 0, axis_index_groups=TEAMS)


def body(rhs, inverse, factor, pattern):
    weight_a = prepare(pattern[0], rhs[0, 0], inverse[0, 0], factor[0, 0])

    with jax.named_scope("gather"):
        left_a, right_a = ring(weight_a, 1), ring(weight_a, -1)
        weight_b, left_b, right_b = [ring(weight_a, steps, True) for steps in (0, 1, -1)]
        pieces = [[weight_a, weight_b, left_a, right_a, left_b, right_b]]
        for _ in range(2):
            left_a, right_a, left_b, right_b = ring(left_a, 1), ring(right_a, -1), ring(left_b, 1), ring(right_b, -1)
            pieces.append([left_a, right_a, left_b, right_b])
        pieces[2] += [ring(left_a, 1), ring(right_b, -1)]
        weights = [part for group in pieces for part in split_weights(group)]
        pieces = [piece for group in pieces for piece in group]
        residue, table = receive(pieces)
        table = table[:, 0, :NB]

    arrived = ()
    for step in range(LEVELS):
        residue, own, other = forward_step(step, table, residue, arrived, weights)
        if step < LEVELS - 1:
            arrived = (hop(other, step, step + 1, 1), hop(own, step, step + 1, 0))

    solved, base = diagonal(residue, pieces)
    turned = turn(weights)
    answer = own
    for level in range(LEVELS - 2, -1, -1):
        other = hop(answer, level + 1, level, 1)
        own = hop(answer, level + 1, level, 0)
        answer = backward_step(level, table, answer, base, own, other, turned)

    with jax.named_scope("collect"):
        home = exchange(jnp.concatenate([solved, answer], axis=1))
        home = jnp.where(half_at(lax.axis_index("chain")) == 1, home[Z:], home[:Z])
    return home[:, :ROWS].reshape(1, 1, LOADS, BLOCK), home[:, ROWS:].reshape(1, 1, LOADS, BLOCK)


def solution(mesh):
    fine = Mesh(mesh.devices.reshape(LEVELS, Y, Z), AXES)
    column = ("y", "z")
    specs = [P("chain", column, *([None] * rank)) for rank in (2, 2, 3, 1)]
    return jax.shard_map(body, mesh=fine, in_specs=tuple(specs), out_specs=(specs[0], specs[0]), check_vma=False)
```

```python
import functools

import jax
import jax.numpy as jnp
from jax import lax
from jax.experimental import pallas as pl
from jax.experimental.pallas import tpu as pltpu
from jax.sharding import Mesh
from jax.sharding import PartitionSpec as P

LEVELS, Y, Z = 8, 4, 8
CLASS = 2 * Z
NB, BLOCK, LOADS = 8, 128, 64
ROWS = LOADS // Z
WIDE = NB * BLOCK
AXES = ("chain", "y", "z")
F32, BF16, I32 = jnp.float32, jnp.bfloat16, jnp.int32
VMEM = pl.BlockSpec(memory_space=pltpu.VMEM)
SMEM = pl.BlockSpec(memory_space=pltpu.SMEM)
HBM = pl.BlockSpec(memory_space=pltpu.HBM)
PARAMS = pltpu.CompilerParams(vmem_limit_bytes=24 << 20)
PIECE = jax.ShapeDtypeStruct((CLASS, ROWS, BLOCK), F32)
PACKED = jax.ShapeDtypeStruct((BLOCK + ROWS, WIDE + BLOCK), F32)
GROUPS = (
    ((0, 0), (0, 1), (-1, 0), (1, 0), (-1, 1), (1, 1)),
    ((-2, 0), (2, 0), (-2, 1), (2, 1)),
    ((-3, 0), (3, 0), (-3, 1), (3, 1), (-4, 0), (4, 1)),
)
HIGHEST = lax.Precision.HIGHEST
CONTRACT_LAST = (((1,), (1,)), ((), ()))


def half_at(level):
    return (level + level // 2) % 2


def half_of(row):
    return (row >= Y // 2).astype(I32) if hasattr(row, "astype") else int(row >= Y // 2)


def side_of(row):
    return ((row == 1) | (row == 2)).astype(I32)


def prepare_kernel(pattern_far, rhs_far, inverse_far, factor_far, piece, pattern, rhs, inverse, factor, arrival):
    copies = [
        pltpu.make_async_copy(source, target, arrival.at[i])
        for i, (source, target) in enumerate(((inverse_far, inverse), (factor_far, factor), (rhs_far, rhs), (pattern_far, pattern)))
    ]
    for copy in copies:
        copy.start()
    place, row, member = lax.axis_index("chain"), lax.axis_index("y"), lax.axis_index("z")
    last = place == LEVELS - 1
    side = side_of(row)
    copies[0].wait()
    turned = inverse[...].T
    piece[:BLOCK, WIDE:] = turned
    copies[1].wait()

    @pl.when(last)
    def _():
        piece[:BLOCK, :BLOCK] = jnp.dot(turned, inverse[...], precision=HIGHEST, preferred_element_type=F32)
        piece[:BLOCK, BLOCK:WIDE] = jnp.zeros((BLOCK, WIDE - BLOCK), F32)

    @pl.when(jnp.logical_not(last))
    def _():
        for k in range(NB):
            piece[:BLOCK, k * BLOCK : (k + 1) * BLOCK] = lax.dot_general(
                turned, factor[k], CONTRACT_LAST, precision=HIGHEST, preferred_element_type=F32
            )

    copies[2].wait()
    copies[3].wait()
    lane = lax.broadcasted_iota(I32, (8, BLOCK), 1)
    marks = jnp.zeros((8, BLOCK), F32)
    for k in range(NB):
        target = pattern[0, k]
        there = lax.div(target, Z)
        seat_number = (side_of(there) ^ side) * CLASS + half_of(there) * Z + lax.rem(target, Z)
        seat_number = jnp.where(last, half_of(row) * Z + member, seat_number)
        marks = jnp.where(lane == k, seat_number.astype(F32), marks)
    piece[BLOCK:, WIDE:] = marks
    for i in range(Z):
        piece[BLOCK:, i * BLOCK : (i + 1) * BLOCK] = rhs[i * ROWS : (i + 1) * ROWS]


def prepare(pattern, rhs, inverse, factor):
    return pl.pallas_call(
        prepare_kernel,
        in_specs=[HBM] * 4,
        out_specs=VMEM,
        out_shape=PACKED,
        scratch_shapes=[
            pltpu.SMEM((1, NB), I32),
            pltpu.VMEM((LOADS, BLOCK), F32),
            pltpu.VMEM((BLOCK, BLOCK), F32),
            pltpu.VMEM((NB, BLOCK, BLOCK), F32),
            pltpu.SemaphoreType.DMA((4,)),
        ],
        compiler_params=PARAMS,
        name="prepare",
    )(pattern, rhs, inverse, factor)


def split(value):
    high = value.astype(BF16)
    return high, (value - high.astype(F32)).astype(BF16)


def split_kernel(count, *refs):
    high, low = refs[count:]
    for i, source in enumerate(refs[:count]):
        high[i], low[i] = split(source[:BLOCK, :WIDE])


def split_weights(pieces):
    shape = jax.ShapeDtypeStruct((len(pieces), BLOCK, WIDE), BF16)
    return pl.pallas_call(
        functools.partial(split_kernel, len(pieces)),
        in_specs=[VMEM] * len(pieces),
        out_specs=[VMEM] * 2,
        out_shape=[shape] * 2,
        compiler_params=PARAMS,
        cost_estimate=pl.CostEstimate(flops=0, transcendentals=0, bytes_accessed=8 * len(pieces) * BLOCK * WIDE),
        name="split_weights",
    )(*pieces)


def number(away, other):
    member = lax.axis_index("z")
    return (half_at(lax.axis_index("chain")) ^ other) * Z + lax.rem(member + (Z + away), Z)


ORDER = [step for group in GROUPS for step in group]


def receive_kernel(*refs):
    pieces, (residue, table) = refs[:-2], refs[-2:]
    mine = pl.ds(pl.multiple_of(lax.axis_index("z") * BLOCK, BLOCK), BLOCK)
    for step, piece in zip(ORDER, pieces):
        residue[number(*step)] = piece[BLOCK:, mine]
        table[number(*step)] = piece[BLOCK:, WIDE:].astype(I32)


def receive(pieces):
    return pl.pallas_call(
        receive_kernel,
        in_specs=[VMEM] * len(pieces),
        out_specs=[VMEM, VMEM],
        out_shape=[PIECE, jax.ShapeDtypeStruct(PIECE.shape, I32)],
        compiler_params=PARAMS,
        name="receive",
    )(*pieces)


def supernodes(weights):
    for group, (high, low) in zip(GROUPS, zip(weights[::2], weights[1::2])):
        for i, (away, other) in enumerate(group):
            yield number(away, other), high.at[i], low.at[i]


def active(level):
    return (lax.axis_index("chain") == level) & (half_of(lax.axis_index("y")) == half_at(level))


def forward_kernel(step, arrivals, table, residue, *refs):
    arrived, weights, (residue_out, own, other, total) = refs[:arrivals], refs[arrivals:-4], refs[-4:]

    @pl.when(jnp.logical_not(active(step)))
    def _():
        residue_out[...] = residue[...]

    @pl.when(active(step))
    def _():
        current = residue[...]
        for piece in arrived:
            current = current - piece[...]
        residue_out[...] = current
        if step < LEVELS - 1:
            total[...] = jnp.zeros_like(total)
        for sup, high, low in supernodes(weights):
            left = jnp.concatenate(split(residue_out[sup]), axis=0)
            if step == LEVELS - 1:
                terms = jnp.dot(left, high[:, :BLOCK], preferred_element_type=F32) + jnp.dot(left, low[:, :BLOCK], preferred_element_type=F32)
                own[sup] = terms[:ROWS] + terms[ROWS:]
                continue
            terms = jnp.dot(left, high[...], preferred_element_type=F32) + jnp.dot(left, low[...], preferred_element_type=F32)
            summed = terms[:ROWS] + terms[ROWS:]
            for k in range(NB):
                total[table[sup, k]] += summed[:, k * BLOCK : (k + 1) * BLOCK]
        if step < LEVELS - 1:
            own[...] = total[:CLASS]
            other[...] = total[CLASS:]


def forward_step(step, table, residue, arrived, weights):
    return pl.pallas_call(
        functools.partial(forward_kernel, step, len(arrived)),
        in_specs=[SMEM] + [VMEM] * (1 + len(arrived) + len(weights)),
        out_specs=[VMEM] * 3,
        out_shape=[PIECE] * 3,
        scratch_shapes=[pltpu.VMEM((2 * CLASS, ROWS, BLOCK), F32)],
        compiler_params=PARAMS,
        name=f"forward_{step}",
    )(table, residue, *arrived, *weights)


def turn_kernel(*refs):
    for source, target in zip(refs[:6], refs[6:]):
        for i in range(source.shape[0]):
            for k in range(NB):
                target[i, k * BLOCK : (k + 1) * BLOCK] = source[i, :, k * BLOCK : (k + 1) * BLOCK].T


def turn(weights):
    return pl.pallas_call(
        turn_kernel,
        in_specs=[VMEM] * len(weights),
        out_specs=[VMEM] * len(weights),
        out_shape=[jax.ShapeDtypeStruct((part.shape[0], WIDE, BLOCK), BF16) for part in weights],
        compiler_params=PARAMS,
        name="turn",
    )(*weights)


def backward_kernel(level, table, before, base, own, other, *refs):
    weights, (answer, picked) = refs[:6], refs[-2:]

    @pl.when(jnp.logical_not(active(level)))
    def _():
        answer[...] = before[...]

    @pl.when(active(level))
    def _():
        for half, source in enumerate((own, other)):
            picked[half * CLASS : (half + 1) * CLASS] = jnp.concatenate(split(source[...]), axis=1)
        for sup, high, low in supernodes(weights):
            left = jnp.concatenate([picked[table[sup, k]] for k in range(NB)], axis=1)
            terms = jnp.dot(left, high[...], preferred_element_type=F32) + jnp.dot(left, low[...], preferred_element_type=F32)
            answer[sup] = base[sup] - (terms[:ROWS] + terms[ROWS:])


def last_backward_kernel(table, before, base, own, other, *refs):
    solved, both, answer, picked = refs[6:]
    backward_kernel(0, table, before, base, own, other, *refs[:6], answer, picked)
    for i in range(CLASS):
        start = i // Z * 2 * ROWS
        both[i % Z, start : start + ROWS] = solved[i]
        both[i % Z, start + ROWS : start + 2 * ROWS] = answer[i]


def last_backward_step(table, before, base, own, other, weights, solved):
    return pl.pallas_call(
        last_backward_kernel,
        in_specs=[SMEM] + [VMEM] * (5 + len(weights)),
        out_specs=VMEM,
        out_shape=jax.ShapeDtypeStruct((Z, 4 * ROWS, BLOCK), F32),
        scratch_shapes=[pltpu.VMEM(PIECE.shape, F32), pltpu.VMEM((2 * CLASS, 2 * ROWS, BLOCK), BF16)],
        compiler_params=PARAMS,
        name="backward_0",
    )(table, before, base, own, other, *weights, solved)


def part_kernel(halves, home, kept, moved):
    half = halves[0]
    for target, chosen in ((kept, half), (moved, 1 - half)):
        for member in range(Z):
            for i in range(2):
                rows = pl.ds(pl.multiple_of((chosen * 2 + i) * ROWS, ROWS), ROWS)
                target[i, member * ROWS : (member + 1) * ROWS] = home[member, rows]


def part(halves, home):
    shape = jax.ShapeDtypeStruct((2, LOADS, BLOCK), F32)
    return pl.pallas_call(
        part_kernel, in_specs=[SMEM, VMEM], out_specs=[VMEM] * 2, out_shape=[shape] * 2, compiler_params=PARAMS, name="part"
    )(halves, home)


def finish_kernel(kept, moved, first, second):
    here = half_of(lax.axis_index("y")) == half_at(lax.axis_index("chain"))

    @pl.when(here)
    def _():
        first[...] = kept[0]
        second[...] = kept[1]

    @pl.when(jnp.logical_not(here))
    def _():
        first[...] = moved[0]
        second[...] = moved[1]


def finish(kept, moved):
    shape = jax.ShapeDtypeStruct((LOADS, BLOCK), F32)
    return pl.pallas_call(
        finish_kernel, in_specs=[VMEM] * 2, out_specs=[VMEM] * 2, out_shape=[shape] * 2, compiler_params=PARAMS, name="finish"
    )(kept, moved)


def backward_step(level, table, before, base, own, other, weights):
    return pl.pallas_call(
        functools.partial(backward_kernel, level),
        in_specs=[SMEM] + [VMEM] * (4 + len(weights)),
        out_specs=VMEM,
        out_shape=PIECE,
        scratch_shapes=[pltpu.VMEM((2 * CLASS, 2 * ROWS, BLOCK), BF16)],
        compiler_params=PARAMS,
        name=f"backward_{level}",
    )(table, before, base, own, other, *weights)


def double(left, right, dims):
    terms = 0.0
    for part in split(right):
        terms += lax.dot_general(jnp.concatenate(split(left), axis=0), part, dims, preferred_element_type=F32)
    return terms[:ROWS] + terms[ROWS:]


def diagonal_kernel(residue, *refs):
    pieces, (solved, base) = refs[:-2], refs[-2:]
    for step, piece in zip(ORDER, pieces):
        sup, turned = number(*step), piece[:BLOCK, WIDE:]
        value = double(residue[sup], turned, (((1,), (0,)), ((), ())))
        solved[sup] = value
        base[sup] = double(value, turned, CONTRACT_LAST)


def diagonal(residue, pieces):
    return pl.pallas_call(
        diagonal_kernel,
        in_specs=[VMEM] * (1 + len(pieces)),
        out_specs=[VMEM] * 2,
        out_shape=[PIECE] * 2,
        compiler_params=PARAMS,
        name="diagonal",
    )(residue, *pieces)


def index(chain, y, z):
    return (chain * Y + y) * Z + z


def seat(level, side):
    return side if half_at(level) == 0 else Y - 1 - side


def hop(value, source, target, cross):
    both = [(first, first + target - source) for first in (source % 4, source % 4 + 4)]
    pairs = [
        (index(first, seat(first, side), z), index(second, seat(second, side ^ cross), z))
        for first, second in both
        if 0 <= second < LEVELS
        for side in range(2)
        for z in range(Z)
    ]
    return lax.ppermute(value, AXES, pairs)


def ring(value, steps, native=False, back=False):
    pairs = []
    for level in range(LEVELS):
        for side in range(2):
            row = seat(level, side)
            source = Y - 1 - row if native else row
            pairs += [(index(level, source, z), index(level, row, (z + steps) % Z))[:: -1 if back else 1] for z in range(Z)]
    return lax.ppermute(value, AXES, pairs)


def body(rhs, inverse, factor, pattern):
    arguments = [pltpu.with_memory_space_constraint(value, pltpu.HBM) for value in (pattern[0], rhs[0, 0], inverse[0, 0], factor[0, 0])]
    weight_a = prepare(*arguments)

    with jax.named_scope("gather"):
        left_a, right_a = ring(weight_a, 1), ring(weight_a, -1)
        weight_b, left_b, right_b = [ring(weight_a, steps, True) for steps in (0, 1, -1)]
        pieces = [[weight_a, weight_b, left_a, right_a, left_b, right_b]]
        for _ in range(2):
            left_a, right_a, left_b, right_b = ring(left_a, 1), ring(right_a, -1), ring(left_b, 1), ring(right_b, -1)
            pieces.append([left_a, right_a, left_b, right_b])
        pieces[2] += [ring(left_a, 1), ring(right_b, -1)]
        weights = [part for group in pieces for part in split_weights(group)]
        pieces = [piece for group in pieces for piece in group]
        residue, table = receive(pieces)
        table = table[:, 0, :NB]

    arrived = ()
    for step in range(LEVELS):
        residue, own, other = forward_step(step, table, residue, arrived, weights)
        if step < LEVELS - 1:
            arrived = (hop(other, step, step + 1, 1), hop(own, step, step + 1, 0))

    solved, base = diagonal(residue, pieces)
    turned = turn(weights)
    answer = own
    for level in range(LEVELS - 2, -1, -1):
        other = hop(answer, level + 1, level, 1)
        own = hop(answer, level + 1, level, 0)
        if level:
            answer = backward_step(level, table, answer, base, own, other, turned)
        else:
            both = last_backward_step(table, answer, base, own, other, turned, solved)

    with jax.named_scope("collect"):
        kept, moved = part(half_at(lax.axis_index("chain"))[None], lax.all_to_all(both, "z", 0, 0))
        first, second = finish(kept, ring(moved, 0, True, True))
    return first[None, None], second[None, None]


def solution(mesh):
    fine = Mesh(mesh.devices.reshape(LEVELS, Y, Z), AXES)
    column = ("y", "z")
    specs = [P("chain", column, *([None] * rank)) for rank in (2, 2, 3, 1)]
    return jax.shard_map(body, mesh=fine, in_specs=tuple(specs), out_specs=(specs[0], specs[0]), check_vma=False)
```

```python
import functools

import jax
import jax.numpy as jnp
from jax import lax
from jax.experimental import pallas as pl
from jax.experimental.pallas import tpu as pltpu
from jax.sharding import Mesh
from jax.sharding import PartitionSpec as P

LEVELS, Y, Z = 8, 4, 8
CLASS = 2 * Z
NB, BLOCK, LOADS = 8, 128, 64
ROWS = LOADS // Z
WIDE = NB * BLOCK
AXES = ("chain", "y", "z")
F32, BF16, I32 = jnp.float32, jnp.bfloat16, jnp.int32
VMEM = pl.BlockSpec(memory_space=pltpu.VMEM)
SMEM = pl.BlockSpec(memory_space=pltpu.SMEM)
HBM = pl.BlockSpec(memory_space=pltpu.HBM)
PARAMS = pltpu.CompilerParams(vmem_limit_bytes=24 << 20)
PIECE = jax.ShapeDtypeStruct((CLASS, ROWS, BLOCK), F32)
PACKED = jax.ShapeDtypeStruct((BLOCK + ROWS, WIDE + BLOCK), F32)
GROUPS = (
    ((0, 0), (0, 1), (-1, 0), (1, 0), (-1, 1), (1, 1)),
    ((-2, 0), (2, 0), (-2, 1), (2, 1)),
    ((-3, 0), (3, 0), (-3, 1), (3, 1), (4, 0), (-4, 1)),
)
HIGHEST = lax.Precision.HIGHEST
CONTRACT_LAST = (((1,), (1,)), ((), ()))


def half_at(level):
    return (level + level // 2) % 2


def half_of(row):
    return (row >= Y // 2).astype(I32) if hasattr(row, "astype") else int(row >= Y // 2)


def side_of(row):
    return ((row == 1) | (row == 2)).astype(I32)


def prepare_kernel(pattern_far, rhs_far, inverse_far, factor_far, piece, pattern, rhs, inverse, factor, arrival):
    copies = [
        pltpu.make_async_copy(source, target, arrival.at[i])
        for i, (source, target) in enumerate(((inverse_far, inverse), (factor_far, factor), (rhs_far, rhs), (pattern_far, pattern)))
    ]
    for copy in copies:
        copy.start()
    place, row, member = lax.axis_index("chain"), lax.axis_index("y"), lax.axis_index("z")
    last = place == LEVELS - 1
    side = side_of(row)
    copies[0].wait()
    turned = inverse[...].T
    piece[:BLOCK, WIDE:] = turned
    copies[1].wait()

    @pl.when(last)
    def _():
        piece[:BLOCK, :BLOCK] = jnp.dot(turned, inverse[...], precision=HIGHEST, preferred_element_type=F32)
        piece[:BLOCK, BLOCK:WIDE] = jnp.zeros((BLOCK, WIDE - BLOCK), F32)

    @pl.when(jnp.logical_not(last))
    def _():
        for k in range(NB):
            piece[:BLOCK, k * BLOCK : (k + 1) * BLOCK] = lax.dot_general(
                turned, factor[k], CONTRACT_LAST, precision=HIGHEST, preferred_element_type=F32
            )

    copies[2].wait()
    copies[3].wait()
    lane = lax.broadcasted_iota(I32, (8, BLOCK), 1)
    marks = jnp.zeros((8, BLOCK), F32)
    for k in range(NB):
        target = pattern[0, k]
        there = lax.div(target, Z)
        seat_number = (side_of(there) ^ side) * CLASS + half_of(there) * Z + lax.rem(target, Z)
        seat_number = jnp.where(last, half_of(row) * Z + member, seat_number)
        marks = jnp.where(lane == k, seat_number.astype(F32), marks)
    piece[BLOCK:, WIDE:] = marks
    for i in range(Z):
        piece[BLOCK:, i * BLOCK : (i + 1) * BLOCK] = rhs[i * ROWS : (i + 1) * ROWS]


def prepare(pattern, rhs, inverse, factor):
    return pl.pallas_call(
        prepare_kernel,
        in_specs=[HBM] * 4,
        out_specs=VMEM,
        out_shape=PACKED,
        scratch_shapes=[
            pltpu.SMEM((1, NB), I32),
            pltpu.VMEM((LOADS, BLOCK), F32),
            pltpu.VMEM((BLOCK, BLOCK), F32),
            pltpu.VMEM((NB, BLOCK, BLOCK), F32),
            pltpu.SemaphoreType.DMA((4,)),
        ],
        compiler_params=PARAMS,
        name="prepare",
    )(pattern, rhs, inverse, factor)


def split(value):
    high = value.astype(BF16)
    return high, (value - high.astype(F32)).astype(BF16)


def split_kernel(count, *refs):
    high, low = refs[count:]
    for i, source in enumerate(refs[:count]):
        high[i], low[i] = split(source[:BLOCK, :WIDE])


def split_weights(pieces):
    shape = jax.ShapeDtypeStruct((len(pieces), BLOCK, WIDE), BF16)
    return pl.pallas_call(
        functools.partial(split_kernel, len(pieces)),
        in_specs=[VMEM] * len(pieces),
        out_specs=[VMEM] * 2,
        out_shape=[shape] * 2,
        compiler_params=PARAMS,
        cost_estimate=pl.CostEstimate(flops=0, transcendentals=0, bytes_accessed=8 * len(pieces) * BLOCK * WIDE),
        name="split_weights",
    )(*pieces)


def number(away, other):
    member = lax.axis_index("z")
    return (half_at(lax.axis_index("chain")) ^ other) * Z + lax.rem(member + (Z + away), Z)


ORDER = [step for group in GROUPS for step in group]


def receive_kernel(*refs):
    pieces, (residue, table) = refs[:-2], refs[-2:]
    mine = pl.ds(pl.multiple_of(lax.axis_index("z") * BLOCK, BLOCK), BLOCK)
    for step, piece in zip(ORDER, pieces):
        residue[number(*step)] = piece[BLOCK:, mine]
        table[number(*step)] = piece[BLOCK:, WIDE:].astype(I32)


def receive(pieces):
    return pl.pallas_call(
        receive_kernel,
        in_specs=[VMEM] * len(pieces),
        out_specs=[VMEM, VMEM],
        out_shape=[PIECE, jax.ShapeDtypeStruct(PIECE.shape, I32)],
        compiler_params=PARAMS,
        name="receive",
    )(*pieces)


def supernodes(weights):
    for group, (high, low) in zip(GROUPS, zip(weights[::2], weights[1::2])):
        for i, (away, other) in enumerate(group):
            yield number(away, other), high.at[i], low.at[i]


def active(level):
    return (lax.axis_index("chain") == level) & (half_of(lax.axis_index("y")) == half_at(level))


def forward_kernel(step, arrivals, table, residue, *refs):
    arrived, weights, (residue_out, own, other, total) = refs[:arrivals], refs[arrivals:-4], refs[-4:]

    @pl.when(jnp.logical_not(active(step)))
    def _():
        residue_out[...] = residue[...]

    @pl.when(active(step))
    def _():
        current = residue[...]
        for piece in arrived:
            current = current - piece[...]
        residue_out[...] = current
        if step < LEVELS - 1:
            total[...] = jnp.zeros_like(total)
        for sup, high, low in supernodes(weights):
            left = jnp.concatenate(split(residue_out[sup]), axis=0)
            if step == LEVELS - 1:
                terms = jnp.dot(left, high[:, :BLOCK], preferred_element_type=F32) + jnp.dot(left, low[:, :BLOCK], preferred_element_type=F32)
                own[sup] = terms[:ROWS] + terms[ROWS:]
                continue
            terms = jnp.dot(left, high[...], preferred_element_type=F32) + jnp.dot(left, low[...], preferred_element_type=F32)
            summed = terms[:ROWS] + terms[ROWS:]
            for k in range(NB):
                total[table[sup, k]] += summed[:, k * BLOCK : (k + 1) * BLOCK]
        if step < LEVELS - 1:
            own[...] = total[:CLASS]
            other[...] = total[CLASS:]


def forward_step(step, table, residue, arrived, weights):
    return pl.pallas_call(
        functools.partial(forward_kernel, step, len(arrived)),
        in_specs=[SMEM] + [VMEM] * (1 + len(arrived) + len(weights)),
        out_specs=[VMEM] * 3,
        out_shape=[PIECE] * 3,
        scratch_shapes=[pltpu.VMEM((2 * CLASS, ROWS, BLOCK), F32)],
        compiler_params=PARAMS,
        name=f"forward_{step}",
    )(table, residue, *arrived, *weights)


def turn_kernel(*refs):
    for source, target in zip(refs[:6], refs[6:]):
        for i in range(source.shape[0]):
            for k in range(NB):
                target[i, k * BLOCK : (k + 1) * BLOCK] = source[i, :, k * BLOCK : (k + 1) * BLOCK].T


def turn(weights):
    return pl.pallas_call(
        turn_kernel,
        in_specs=[VMEM] * len(weights),
        out_specs=[VMEM] * len(weights),
        out_shape=[jax.ShapeDtypeStruct((part.shape[0], WIDE, BLOCK), BF16) for part in weights],
        compiler_params=PARAMS,
        name="turn",
    )(*weights)


def backward_kernel(level, table, before, base, own, other, *refs):
    weights, (answer, picked) = refs[:6], refs[-2:]

    @pl.when(jnp.logical_not(active(level)))
    def _():
        answer[...] = before[...]

    @pl.when(active(level))
    def _():
        for half, source in enumerate((own, other)):
            picked[half * CLASS : (half + 1) * CLASS] = jnp.concatenate(split(source[...]), axis=1)
        for sup, high, low in supernodes(weights):
            left = jnp.concatenate([picked[table[sup, k]] for k in range(NB)], axis=1)
            terms = jnp.dot(left, high[...], preferred_element_type=F32) + jnp.dot(left, low[...], preferred_element_type=F32)
            answer[sup] = base[sup] - (terms[:ROWS] + terms[ROWS:])


def last_backward_kernel(table, before, base, own, other, *refs):
    solved, both, answer, picked = refs[6:]
    backward_kernel(0, table, before, base, own, other, *refs[:6], answer, picked)
    for i in range(CLASS):
        start = i // Z * 2 * ROWS
        both[i % Z, start : start + ROWS] = solved[i]
        both[i % Z, start + ROWS : start + 2 * ROWS] = answer[i]


def last_backward_step(table, before, base, own, other, weights, solved):
    return pl.pallas_call(
        last_backward_kernel,
        in_specs=[SMEM] + [VMEM] * (5 + len(weights)),
        out_specs=VMEM,
        out_shape=jax.ShapeDtypeStruct((Z, 4 * ROWS, BLOCK), F32),
        scratch_shapes=[pltpu.VMEM(PIECE.shape, F32), pltpu.VMEM((2 * CLASS, 2 * ROWS, BLOCK), BF16)],
        compiler_params=PARAMS,
        name="backward_0",
    )(table, before, base, own, other, *weights, solved)


def part_kernel(halves, home, kept, moved):
    half = halves[0]
    for target, chosen in ((kept, half), (moved, 1 - half)):
        for member in range(Z):
            for i in range(2):
                rows = pl.ds(pl.multiple_of((chosen * 2 + i) * ROWS, ROWS), ROWS)
                target[i, member * ROWS : (member + 1) * ROWS] = home[member, rows]


def part(halves, home):
    shape = jax.ShapeDtypeStruct((2, LOADS, BLOCK), F32)
    return pl.pallas_call(
        part_kernel, in_specs=[SMEM, VMEM], out_specs=[VMEM] * 2, out_shape=[shape] * 2, compiler_params=PARAMS, name="part"
    )(halves, home)


def finish_kernel(kept, moved, first, second):
    here = half_of(lax.axis_index("y")) == half_at(lax.axis_index("chain"))

    @pl.when(here)
    def _():
        first[...] = kept[0]
        second[...] = kept[1]

    @pl.when(jnp.logical_not(here))
    def _():
        first[...] = moved[0]
        second[...] = moved[1]


def finish(kept, moved):
    shape = jax.ShapeDtypeStruct((LOADS, BLOCK), F32)
    return pl.pallas_call(
        finish_kernel, in_specs=[VMEM] * 2, out_specs=[VMEM] * 2, out_shape=[shape] * 2, compiler_params=PARAMS, name="finish"
    )(kept, moved)


def backward_step(level, table, before, base, own, other, weights):
    return pl.pallas_call(
        functools.partial(backward_kernel, level),
        in_specs=[SMEM] + [VMEM] * (4 + len(weights)),
        out_specs=VMEM,
        out_shape=PIECE,
        scratch_shapes=[pltpu.VMEM((2 * CLASS, 2 * ROWS, BLOCK), BF16)],
        compiler_params=PARAMS,
        name=f"backward_{level}",
    )(table, before, base, own, other, *weights)


def double(left, right, dims):
    terms = 0.0
    for part in split(right):
        terms += lax.dot_general(jnp.concatenate(split(left), axis=0), part, dims, preferred_element_type=F32)
    return terms[:ROWS] + terms[ROWS:]


def diagonal_kernel(residue, *refs):
    pieces, (solved, base) = refs[:-2], refs[-2:]
    for step, piece in zip(ORDER, pieces):
        sup, turned = number(*step), piece[:BLOCK, WIDE:]
        value = double(residue[sup], turned, (((1,), (0,)), ((), ())))
        solved[sup] = value
        base[sup] = double(value, turned, CONTRACT_LAST)


def diagonal(residue, pieces):
    return pl.pallas_call(
        diagonal_kernel,
        in_specs=[VMEM] * (1 + len(pieces)),
        out_specs=[VMEM] * 2,
        out_shape=[PIECE] * 2,
        compiler_params=PARAMS,
        name="diagonal",
    )(residue, *pieces)


def index(chain, y, z):
    return (chain * Y + y) * Z + z


def seat(level, side):
    return side if half_at(level) == 0 else Y - 1 - side


def hop(value, source, target, cross):
    both = [(first, first + target - source) for first in (source % 4, source % 4 + 4)]
    pairs = [
        (index(first, seat(first, side), z), index(second, seat(second, side ^ cross), z))
        for first, second in both
        if 0 <= second < LEVELS
        for side in range(2)
        for z in range(Z)
    ]
    return lax.ppermute(value, AXES, pairs)


def ring(value, steps, native=False, back=False):
    pairs = []
    for level in range(LEVELS):
        for side in range(2):
            row = seat(level, side)
            source = Y - 1 - row if native else row
            pairs += [(index(level, source, z), index(level, row, (z + steps) % Z))[:: -1 if back else 1] for z in range(Z)]
    return lax.ppermute(value, AXES, pairs)


def body(rhs, inverse, factor, pattern):
    arguments = [pltpu.with_memory_space_constraint(value, pltpu.HBM) for value in (pattern[0], rhs[0, 0], inverse[0, 0], factor[0, 0])]
    weight_a = prepare(*arguments)

    with jax.named_scope("gather"):
        left_a, right_a = ring(weight_a, 1), ring(weight_a, -1)
        weight_b, left_b, right_b = [ring(weight_a, steps, True) for steps in (0, 1, -1)]
        pieces = [[weight_a, weight_b, left_a, right_a, left_b, right_b]]
        for _ in range(2):
            left_a, right_a, left_b, right_b = ring(left_a, 1), ring(right_a, -1), ring(left_b, 1), ring(right_b, -1)
            pieces.append([left_a, right_a, left_b, right_b])
        pieces[2] += [ring(right_a, -1), ring(left_b, 1)]
        weights = [part for group in pieces for part in split_weights(group)]
        pieces = [piece for group in pieces for piece in group]
        residue, table = receive(pieces)
        table = table[:, 0, :NB]

    arrived = ()
    for step in range(LEVELS):
        residue, own, other = forward_step(step, table, residue, arrived, weights)
        if step < LEVELS - 1:
            arrived = (hop(other, step, step + 1, 1), hop(own, step, step + 1, 0))

    solved, base = diagonal(residue, pieces)
    turned = turn(weights)
    answer = own
    for level in range(LEVELS - 2, -1, -1):
        other = hop(answer, level + 1, level, 1)
        own = hop(answer, level + 1, level, 0)
        if level:
            answer = backward_step(level, table, answer, base, own, other, turned)
        else:
            both = last_backward_step(table, answer, base, own, other, turned, solved)

    with jax.named_scope("collect"):
        kept, moved = part(half_at(lax.axis_index("chain"))[None], lax.all_to_all(both, "z", 0, 0))
        first, second = finish(kept, ring(moved, 0, True, True))
    return first[None, None], second[None, None]


def solution(mesh):
    fine = Mesh(mesh.devices.reshape(LEVELS, Y, Z), AXES)
    column = ("y", "z")
    specs = [P("chain", column, *([None] * rank)) for rank in (2, 2, 3, 1)]
    return jax.shard_map(body, mesh=fine, in_specs=tuple(specs), out_specs=(specs[0], specs[0]), check_vma=False)
```

```python
import functools

import jax
import jax.numpy as jnp
from jax import lax
from jax.experimental import pallas as pl
from jax.experimental.pallas import tpu as pltpu
from jax.sharding import Mesh
from jax.sharding import PartitionSpec as P

LEVELS, Y, Z = 8, 4, 8
CLASS = 2 * Z
NB, BLOCK, LOADS = 8, 128, 64
ROWS = LOADS // Z
WIDE = NB * BLOCK
AXES = ("chain", "y", "z")
F32, BF16, I32 = jnp.float32, jnp.bfloat16, jnp.int32
VMEM = pl.BlockSpec(memory_space=pltpu.VMEM)
SMEM = pl.BlockSpec(memory_space=pltpu.SMEM)
HBM = pl.BlockSpec(memory_space=pltpu.HBM)
PARAMS = pltpu.CompilerParams(vmem_limit_bytes=24 << 20)
PIECE = jax.ShapeDtypeStruct((CLASS, ROWS, BLOCK), F32)
PACKED = jax.ShapeDtypeStruct((BLOCK + ROWS, WIDE + BLOCK), F32)
GROUPS = (
    ((0, 0), (0, 1), (-1, 0), (1, 0), (-1, 1), (1, 1)),
    ((-2, 0), (2, 0), (-2, 1), (2, 1)),
    ((-3, 0), (3, 0), (-3, 1), (3, 1), (-4, 0), (4, 1)),
)
HIGHEST = lax.Precision.HIGHEST
CONTRACT_LAST = (((1,), (1,)), ((), ()))


def half_at(level):
    return (level + level // 2) % 2


def half_of(row):
    return (row >= Y // 2).astype(I32) if hasattr(row, "astype") else int(row >= Y // 2)


def side_of(row):
    return ((row == 1) | (row == 2)).astype(I32)


def prepare_kernel(pattern_far, rhs_far, inverse_far, factor_far, piece, pattern, rhs, inverse, factor, arrival):
    copies = [
        pltpu.make_async_copy(source, target, arrival.at[i])
        for i, (source, target) in enumerate(((inverse_far, inverse), (factor_far, factor), (rhs_far, rhs), (pattern_far, pattern)))
    ]
    for copy in copies:
        copy.start()
    place, row, member = lax.axis_index("chain"), lax.axis_index("y"), lax.axis_index("z")
    last = place == LEVELS - 1
    side = side_of(row)
    copies[0].wait()
    turned = inverse[...].T
    piece[:BLOCK, WIDE:] = turned
    copies[1].wait()

    @pl.when(last)
    def _():
        piece[:BLOCK, :BLOCK] = jnp.dot(turned, inverse[...], precision=HIGHEST, preferred_element_type=F32)
        piece[:BLOCK, BLOCK:WIDE] = jnp.zeros((BLOCK, WIDE - BLOCK), F32)

    @pl.when(jnp.logical_not(last))
    def _():
        for k in range(NB):
            piece[:BLOCK, k * BLOCK : (k + 1) * BLOCK] = lax.dot_general(
                turned, factor[k], CONTRACT_LAST, precision=HIGHEST, preferred_element_type=F32
            )

    copies[2].wait()
    copies[3].wait()
    lane = lax.broadcasted_iota(I32, (8, BLOCK), 1)
    marks = jnp.zeros((8, BLOCK), F32)
    for k in range(NB):
        target = pattern[0, k]
        there = lax.div(target, Z)
        seat_number = (side_of(there) ^ side) * CLASS + half_of(there) * Z + lax.rem(target, Z)
        seat_number = jnp.where(last, half_of(row) * Z + member, seat_number)
        marks = jnp.where(lane == k, seat_number.astype(F32), marks)
    piece[BLOCK:, WIDE:] = marks
    for i in range(Z):
        piece[BLOCK:, i * BLOCK : (i + 1) * BLOCK] = rhs[i * ROWS : (i + 1) * ROWS]


def prepare(pattern, rhs, inverse, factor):
    return pl.pallas_call(
        prepare_kernel,
        in_specs=[HBM] * 4,
        out_specs=VMEM,
        out_shape=PACKED,
        scratch_shapes=[
            pltpu.SMEM((1, NB), I32),
            pltpu.VMEM((LOADS, BLOCK), F32),
            pltpu.VMEM((BLOCK, BLOCK), F32),
            pltpu.VMEM((NB, BLOCK, BLOCK), F32),
            pltpu.SemaphoreType.DMA((4,)),
        ],
        compiler_params=PARAMS,
        name="prepare",
    )(pattern, rhs, inverse, factor)


def split(value):
    high = value.astype(BF16)
    return high, (value - high.astype(F32)).astype(BF16)


def split_kernel(*refs):
    for i, source in enumerate(refs[:-1]):
        refs[-1][i, :BLOCK], refs[-1][i, BLOCK:] = split(source[:BLOCK, :WIDE])


def split_weights(pieces):
    shape = jax.ShapeDtypeStruct((len(pieces), 2 * BLOCK, WIDE), BF16)
    return pl.pallas_call(
        split_kernel,
        in_specs=[VMEM] * len(pieces),
        out_specs=VMEM,
        out_shape=shape,
        compiler_params=PARAMS,
        cost_estimate=pl.CostEstimate(flops=0, transcendentals=0, bytes_accessed=8 * len(pieces) * BLOCK * WIDE),
        name="split_weights",
    )(*pieces)


def number(away, other):
    member = lax.axis_index("z")
    return (half_at(lax.axis_index("chain")) ^ other) * Z + lax.rem(member + (Z + away), Z)


ORDER = [step for group in GROUPS for step in group]


def receive_kernel(*refs):
    pieces, (residue, table) = refs[:-2], refs[-2:]
    mine = pl.ds(pl.multiple_of(lax.axis_index("z") * BLOCK, BLOCK), BLOCK)
    for step, piece in zip(ORDER, pieces):
        residue[number(*step)] = piece[BLOCK:, mine]
        table[number(*step)] = piece[BLOCK:, WIDE:].astype(I32)


def receive(pieces):
    return pl.pallas_call(
        receive_kernel,
        in_specs=[VMEM] * len(pieces),
        out_specs=[VMEM, VMEM],
        out_shape=[PIECE, jax.ShapeDtypeStruct(PIECE.shape, I32)],
        compiler_params=PARAMS,
        name="receive",
    )(*pieces)


def supernodes(weights):
    for group, blocks in zip(GROUPS, weights):
        for i, (away, other) in enumerate(group):
            yield number(away, other), blocks.at[i]


def active(level):
    return (lax.axis_index("chain") == level) & (half_of(lax.axis_index("y")) == half_at(level))


def forward_kernel(step, arrivals, table, residue, *refs):
    arrived, weights, (residue_out, own, other, *totals) = refs[:arrivals], refs[arrivals:-5], refs[-5:]

    @pl.when(jnp.logical_not(active(step)))
    def _():
        residue_out[...] = residue[...]

    @pl.when(active(step))
    def _():
        current = residue[...]
        for piece in arrived:
            current = current - piece[...]
        residue_out[...] = current
        if step < LEVELS - 1:
            for total in totals:
                total[...] = jnp.zeros_like(total)
        for count, (sup, blocks) in enumerate(supernodes(weights)):
            left = jnp.concatenate(split(residue_out[sup]), axis=0)
            left = jnp.concatenate([left, left], axis=1)
            if step == LEVELS - 1:
                terms = jnp.dot(left, blocks[:, :BLOCK], preferred_element_type=F32)
                own[sup] = terms[:ROWS] + terms[ROWS:]
                continue
            terms = jnp.dot(left, blocks[...], preferred_element_type=F32)
            summed = terms[:ROWS] + terms[ROWS:]
            targets = [table[sup, k] for k in range(NB)]
            total = totals[count % len(totals)]
            sums = [total[targets[k]] + summed[:, k * BLOCK : (k + 1) * BLOCK] for k in range(NB)]
            for target, value in zip(targets, sums):
                total[target] = value
        if step < LEVELS - 1:
            own[...] = totals[0][:CLASS] + totals[1][:CLASS]
            other[...] = totals[0][CLASS:] + totals[1][CLASS:]


def forward_step(step, table, residue, arrived, weights):
    return pl.pallas_call(
        functools.partial(forward_kernel, step, len(arrived)),
        in_specs=[SMEM] + [VMEM] * (1 + len(arrived) + len(weights)),
        out_specs=[VMEM] * 3,
        out_shape=[PIECE] * 3,
        scratch_shapes=[pltpu.VMEM((2 * CLASS, ROWS, BLOCK), F32)] * 2,
        compiler_params=PARAMS,
        name=f"forward_{step}",
    )(table, residue, *arrived, *weights)


def turn_kernel(*refs):
    for source, target in zip(refs[:3], refs[3:]):
        for i in range(source.shape[0]):
            for k in range(NB):
                for part in (slice(BLOCK), slice(BLOCK, 2 * BLOCK)):
                    target[i, k * BLOCK : (k + 1) * BLOCK, part] = source[i, part, k * BLOCK : (k + 1) * BLOCK].T


def turn(weights):
    return pl.pallas_call(
        turn_kernel,
        in_specs=[VMEM] * len(weights),
        out_specs=[VMEM] * len(weights),
        out_shape=[jax.ShapeDtypeStruct((part.shape[0], WIDE, 2 * BLOCK), BF16) for part in weights],
        compiler_params=PARAMS,
        name="turn",
    )(*weights)


def backward_kernel(level, table, before, base, own, other, *refs):
    weights, (answer, picked) = refs[:3], refs[-2:]

    @pl.when(jnp.logical_not(active(level)))
    def _():
        answer[...] = before[...]

    @pl.when(active(level))
    def _():
        for half, source in enumerate((own, other)):
            picked[half * CLASS : (half + 1) * CLASS] = jnp.concatenate(split(source[...]), axis=1)
        for sup, blocks in supernodes(weights):
            left = jnp.concatenate([picked[table[sup, k]] for k in range(NB)], axis=1)
            terms = jnp.dot(left, blocks[...], preferred_element_type=F32)
            terms = terms[:, :BLOCK] + terms[:, BLOCK:]
            answer[sup] = base[sup] - (terms[:ROWS] + terms[ROWS:])


def last_backward_kernel(table, before, base, own, other, *refs):
    solved, both, answer, picked = refs[3:]
    backward_kernel(0, table, before, base, own, other, *refs[:3], answer, picked)
    for i in range(CLASS):
        start = i // Z * 2 * ROWS
        both[i % Z, start : start + ROWS] = solved[i]
        both[i % Z, start + ROWS : start + 2 * ROWS] = answer[i]


def last_backward_step(table, before, base, own, other, weights, solved):
    return pl.pallas_call(
        last_backward_kernel,
        in_specs=[SMEM] + [VMEM] * (5 + len(weights)),
        out_specs=VMEM,
        out_shape=jax.ShapeDtypeStruct((Z, 4 * ROWS, BLOCK), F32),
        scratch_shapes=[pltpu.VMEM(PIECE.shape, F32), pltpu.VMEM((2 * CLASS, 2 * ROWS, BLOCK), BF16)],
        compiler_params=PARAMS,
        name="backward_0",
    )(table, before, base, own, other, *weights, solved)


def part_kernel(halves, home, kept, moved):
    half = halves[0]
    for target, chosen in ((kept, half), (moved, 1 - half)):
        for member in range(Z):
            for i in range(2):
                rows = pl.ds(pl.multiple_of((chosen * 2 + i) * ROWS, ROWS), ROWS)
                target[i, member * ROWS : (member + 1) * ROWS] = home[member, rows]


def part(halves, home):
    shape = jax.ShapeDtypeStruct((2, LOADS, BLOCK), F32)
    return pl.pallas_call(
        part_kernel, in_specs=[SMEM, VMEM], out_specs=[VMEM] * 2, out_shape=[shape] * 2, compiler_params=PARAMS, name="part"
    )(halves, home)


def finish_kernel(kept, moved, first, second):
    here = half_of(lax.axis_index("y")) == half_at(lax.axis_index("chain"))

    @pl.when(here)
    def _():
        first[...] = kept[0]
        second[...] = kept[1]

    @pl.when(jnp.logical_not(here))
    def _():
        first[...] = moved[0]
        second[...] = moved[1]


def finish(kept, moved):
    shape = jax.ShapeDtypeStruct((LOADS, BLOCK), F32)
    return pl.pallas_call(
        finish_kernel, in_specs=[VMEM] * 2, out_specs=[VMEM] * 2, out_shape=[shape] * 2, compiler_params=PARAMS, name="finish"
    )(kept, moved)


def backward_step(level, table, before, base, own, other, weights):
    return pl.pallas_call(
        functools.partial(backward_kernel, level),
        in_specs=[SMEM] + [VMEM] * (4 + len(weights)),
        out_specs=VMEM,
        out_shape=PIECE,
        scratch_shapes=[pltpu.VMEM((2 * CLASS, 2 * ROWS, BLOCK), BF16)],
        compiler_params=PARAMS,
        name=f"backward_{level}",
    )(table, before, base, own, other, *weights)


def double(left, right, dims):
    terms = 0.0
    for part in split(right):
        terms += lax.dot_general(jnp.concatenate(split(left), axis=0), part, dims, preferred_element_type=F32)
    return terms[:ROWS] + terms[ROWS:]


def diagonal_kernel(residue, *refs):
    pieces, (solved, base) = refs[:-2], refs[-2:]
    for step, piece in zip(ORDER, pieces):
        sup, turned = number(*step), piece[:BLOCK, WIDE:]
        value = double(residue[sup], turned, (((1,), (0,)), ((), ())))
        solved[sup] = value
        base[sup] = double(value, turned, CONTRACT_LAST)


def diagonal(residue, pieces):
    return pl.pallas_call(
        diagonal_kernel,
        in_specs=[VMEM] * (1 + len(pieces)),
        out_specs=[VMEM] * 2,
        out_shape=[PIECE] * 2,
        compiler_params=PARAMS,
        name="diagonal",
    )(residue, *pieces)


def index(chain, y, z):
    return (chain * Y + y) * Z + z


def seat(level, side):
    return side if half_at(level) == 0 else Y - 1 - side


def hop(value, source, target, cross):
    both = [(first, first + target - source) for first in (source % 4, source % 4 + 4)]
    pairs = [
        (index(first, seat(first, side), z), index(second, seat(second, side ^ cross), z))
        for first, second in both
        if 0 <= second < LEVELS
        for side in range(2)
        for z in range(Z)
    ]
    return lax.ppermute(value, AXES, pairs)


def ring(value, steps, native=False, back=False):
    pairs = []
    for level in range(LEVELS):
        for side in range(2):
            row = seat(level, side)
            source = Y - 1 - row if native else row
            pairs += [(index(level, source, z), index(level, row, (z + steps) % Z))[:: -1 if back else 1] for z in range(Z)]
    return lax.ppermute(value, AXES, pairs)


def body(rhs, inverse, factor, pattern):
    arguments = [pltpu.with_memory_space_constraint(value, pltpu.HBM) for value in (pattern[0], rhs[0, 0], inverse[0, 0], factor[0, 0])]
    weight_a = prepare(*arguments)

    with jax.named_scope("gather"):
        left_a, right_a = ring(weight_a, 1), ring(weight_a, -1)
        weight_b, left_b, right_b = [ring(weight_a, steps, True) for steps in (0, 1, -1)]
        pieces = [[weight_a, weight_b, left_a, right_a, left_b, right_b]]
        for _ in range(2):
            left_a, right_a, left_b, right_b = ring(left_a, 1), ring(right_a, -1), ring(left_b, 1), ring(right_b, -1)
            pieces.append([left_a, right_a, left_b, right_b])
        pieces[2] += [ring(left_a, 1), ring(right_b, -1)]
        weights = [split_weights(group) for group in pieces]
        pieces = [piece for group in pieces for piece in group]
        residue, table = receive(pieces)
        table = table[:, 0, :NB]

    arrived = ()
    for step in range(LEVELS):
        residue, own, other = forward_step(step, table, residue, arrived, weights)
        if step < LEVELS - 1:
            arrived = (hop(other, step, step + 1, 1), hop(own, step, step + 1, 0))

    solved, base = diagonal(residue, pieces)
    turned = turn(weights)
    answer = own
    for level in range(LEVELS - 2, -1, -1):
        other = hop(answer, level + 1, level, 1)
        own = hop(answer, level + 1, level, 0)
        if level:
            answer = backward_step(level, table, answer, base, own, other, turned)
        else:
            both = last_backward_step(table, answer, base, own, other, turned, solved)

    with jax.named_scope("collect"):
        kept, moved = part(half_at(lax.axis_index("chain"))[None], lax.all_to_all(both, "z", 0, 0))
        first, second = finish(kept, ring(moved, 0, True, True))
    return first[None, None], second[None, None]


def solution(mesh):
    fine = Mesh(mesh.devices.reshape(LEVELS, Y, Z), AXES)
    column = ("y", "z")
    specs = [P("chain", column, *([None] * rank)) for rank in (2, 2, 3, 1)]
    return jax.shard_map(body, mesh=fine, in_specs=tuple(specs), out_specs=(specs[0], specs[0]), check_vma=False)
```
